32 devices in a mesh: dp: 8 (over y, x, core), mp: 4 (over z).
Axes of the slice: x: 2, y: 2, z: 4, core: 2. Of those that a mesh axis runs over, the one named last changes fastest.
Arguments:
- inputs: bfloat16 [8192, 2048], P(('dp', 'mp')), may hold values from -6 to 6
- w_query: bfloat16 [2048, 2048], P('dp', 'mp'), may hold values from -0.125 to 0.125
- w_key: bfloat16 [2048, 2048], P('dp', 'mp'), may hold values from -0.125 to 0.125
- w_value: bfloat16 [2048, 2048], P('dp', 'mp'), may hold values from -0.125 to 0.125
- q_gain: bfloat16 [16, 128], P('mp', 'dp'), may hold values from 1 to 8
- k_gain: bfloat16 [16, 128], P('mp', 'dp'), may hold values from 1 to 8
- w_out: bfloat16 [2048, 2048], P('mp', 'dp'), may hold values from -0.125 to 0.125
- attn_gain: bfloat16 [2048], P('dp'), may hold values from 0.099609375 to 1.8984375
- w_gate: bfloat16 [2048, 8192], P('dp', 'mp'), may hold values from -0.125 to 0.125
- w_up: bfloat16 [2048, 8192], P('dp', 'mp'), may hold values from -0.125 to 0.125
- w_down: bfloat16 [8192, 2048], P('mp', 'dp'), may hold values from -0.0625 to 0.0625
- mlp_gain: bfloat16 [2048], P('dp'), may hold values from 0.099609375 to 1.8984375
- cotangent: bfloat16 [8192, 2048], P(('dp', 'mp')), may hold values from -6 to 6
Outputs:
- output: float32 [8192, 2048], P(('dp', 'mp'))
- input_grad: float32 [8192, 2048], P(('dp', 'mp'))
- grad_w_query: float32 [2048, 2048], P('dp', 'mp')
- grad_w_key: float32 [2048, 2048], P('dp', 'mp')
- grad_w_value: float32 [2048, 2048], P('dp', 'mp')
- grad_q_gain: float32 [16, 128], P('mp', 'dp')
- grad_k_gain: float32 [16, 128], P('mp', 'dp')
- grad_w_out: float32 [2048, 2048], P('mp', 'dp')
- grad_attn_gain: float32 [2048], P('dp')
- grad_w_gate: float32 [2048, 8192], P('dp', 'mp')
- grad_w_up: float32 [2048, 8192], P('dp', 'mp')
- grad_w_down: float32 [8192, 2048], P('mp', 'dp')
- grad_mlp_gain: float32 [2048], P('dp')
The draws below stay inside these ranges and needn't reach their ends.
All inputs are finite; a program needn't handle non-finite values.
Results may differ from the reference program's by a relative error of at most 0.02.
The reference program's roundings to bfloat16 on the way count: a program that leaves them out, or rounds other values in their place, can miss the bound.
Values may be sent and summed in bfloat16 or wider, within the bound.
No kernel may reach another device: no remote copies, remote signals or barrier semaphores. Data moves between devices by JAX's collectives and lax.ppermute only.
A program may use at most 320 MiB of HBM per device.

```python
import jax
import jax.numpy as jnp
from jax import lax

D = 2048
H = 16
HD = 128
FF = 8192
L = 1024
TOKENS = 8192


def head_gain(key):
    column = jax.random.uniform(jax.random.fold_in(key, 3), (H, HD), jnp.float32, 1.0, 2.0)
    return column.astype(jnp.bfloat16)


def draw_q_gain(key, part):
    return head_gain(jax.random.fold_in(key, 17))


def draw_k_gain(key, part):
    return head_gain(jax.random.fold_in(key, 29))


def spiked(result, key, source, target, parts, factor):
    def block_of(dim):
        return (jnp.arange(result.shape[dim]) // (result.shape[dim] // parts)).reshape((-1,) + (1,) * (result.ndim - 1 - dim))

    near = jax.random.permutation(key, parts)[block_of(target)]
    other_side = (block_of(target) + parts // 2) % parts
    return jnp.where((block_of(source) == near) | (block_of(source) == other_side), factor * result, result)


def block_levels(stream_key, extent, split, smallest, high):
    loudness = 1.0
    for axis_at, shards_of in split:
        draws = jax.random.uniform(jax.random.fold_in(jax.random.fold_in(stream_key, 6), axis_at), (shards_of,), jnp.float32, smallest / len(split), high / len(split))
        loudness = loudness * jnp.repeat(jnp.exp(draws), extent[axis_at] // shards_of).reshape((-1,) + (1,) * (len(extent) - 1 - axis_at))
    return loudness


def scatter_about(rng, dims, spread, reach, split=(), held_as=jnp.bfloat16):
    gain = block_levels(rng, dims, split, -0.22, 0.18) if split else 1.0
    drawn = jax.random.normal(rng, dims, jnp.float32) * spread * gain
    return jnp.minimum(jnp.maximum(drawn, -reach), reach).astype(held_as)


def heavy_noise(key, extent, width, reach, shards, heavy, held_as=jnp.bfloat16):
    result = width * jax.random.normal(key, extent, jnp.float32)
    if shards:
        result = result * block_levels(key, extent, shards, -0.22, 0.18)
    return jnp.clip(spiked(result, jax.random.fold_in(key, 3), *heavy), -reach, reach).astype(held_as)


def setup_inputs(seed: int = 0) -> dict:
    seeds = jax.random.split(jax.random.key(seed), 14)
    inputs = heavy_noise(seeds[0], (TOKENS, D), 1.0, 6.0, ((0, 32),), (0, 1, 32, 2.75))
    w_query = scatter_about(seeds[1], (D, D), D ** -0.5, 0.125, ((0, 8), (1, 4)))
    w_key = scatter_about(seeds[2], (D, D), D ** -0.5, 0.125, ((0, 8), (1, 4)))
    w_value = scatter_about(seeds[3], (D, D), D ** -0.5, 0.125, ((0, 8), (1, 4)))
    q_gain = draw_q_gain(jax.random.fold_in(seeds[13], 71), 0)
    k_gain = draw_k_gain(jax.random.fold_in(seeds[13], 71), 0)
    w_out = scatter_about(seeds[6], (D, D), D ** -0.5, 0.125, ((0, 4), (1, 8)))
    attn_gain = jnp.clip(1.0 + 0.18 * jax.random.normal(seeds[7], (D,), jnp.float32), 0.099609375, 1.8984375).astype(jnp.bfloat16)
    w_gate = scatter_about(seeds[8], (D, FF), D ** -0.5, 0.125, ((0, 8), (1, 4)))
    w_up = scatter_about(seeds[9], (D, FF), D ** -0.5, 0.125, ((0, 8), (1, 4)))
    w_down = scatter_about(seeds[10], (FF, D), FF ** -0.5, 0.0625, ((0, 4), (1, 8)))
    mlp_gain = jnp.clip(1.0 + 0.18 * jax.random.normal(seeds[11], (D,), jnp.float32), 0.099609375, 1.8984375).astype(jnp.bfloat16)
    cotangent = heavy_noise(seeds[12], (TOKENS, D), 1.0, 6.0, ((0, 32),), (0, 1, 32, 2.75))
    return dict(inputs=inputs, w_query=w_query, w_key=w_key, w_value=w_value, q_gain=q_gain, k_gain=k_gain, w_out=w_out, attn_gain=attn_gain, w_gate=w_gate, w_up=w_up, w_down=w_down, mlp_gain=mlp_gain, cotangent=cotangent)


epsilon = 1e-06
rope_base = 500000.0
block_rows = 512

def dot_plain(left, right):
    return jnp.dot(left, right, preferred_element_type=jnp.float32)

def dot_right_t(left, right):
    return lax.dot_general(left, right, (((1,), (1,)), ((), ())), preferred_element_type=jnp.float32)

def dot_left_t(left, right):
    return lax.dot_general(left, right, (((0,), (0,)), ((), ())), preferred_element_type=jnp.float32)

def rope_tables(rows, length, head):
    half = head // 2
    freqs = rope_base ** (-2.0 * jnp.arange(half, dtype=jnp.float32) / head)
    places = (jnp.arange(rows) % length).astype(jnp.float32)
    angles = places[:, None] * freqs[None, :]
    return (jnp.cos(angles)[:, None, :], jnp.sin(angles)[:, None, :])

def rotate(values, cosine, sine, sign):
    half = values.shape[-1] // 2
    first = values[..., :half]
    second = values[..., half:]
    return jnp.concatenate([first * cosine - sign * (second * sine), second * cosine + sign * (first * sine)], axis=-1)

def causal_scores(queries, keys, first, last):
    block = last - first
    scale = queries.shape[-1] ** (-0.5)
    scores = jnp.einsum('sqhd,skhd->shqk', queries[:, first:last], keys[:, :last], preferred_element_type=jnp.float32) * scale
    allowed = jnp.arange(last)[None, :] <= (first + jnp.arange(block))[:, None]
    return jnp.where(allowed, scores, -1e+30)

def attend(queries, keys, values):
    length = queries.shape[1]
    block = min(block_rows, length)
    outs = []
    sums = []
    for first in range(0, length, block):
        last = first + block
        scores = causal_scores(queries, keys, first, last)
        peak = lax.optimization_barrier(jnp.max(scores, axis=-1, keepdims=True))
        total = jnp.log(lax.optimization_barrier(jnp.sum(jnp.exp(scores - peak), axis=-1, keepdims=True))) + peak
        probs = jnp.exp(scores - total).astype(jnp.bfloat16)
        outs.append(jnp.einsum('shqk,skhd->sqhd', probs, values[:, :last], preferred_element_type=jnp.float32).astype(jnp.bfloat16))
        sums.append(total)
    return (jnp.concatenate(outs, axis=1), jnp.concatenate(sums, axis=2))

def attend_back(queries, keys, values, sums, grads):
    length = queries.shape[1]
    block = min(block_rows, length)
    scale = queries.shape[-1] ** (-0.5)
    d_keys = jnp.zeros(keys.shape, jnp.float32)
    d_values = jnp.zeros(values.shape, jnp.float32)
    d_queries = []
    for first in range(0, length, block):
        last = first + block
        scores = causal_scores(queries, keys, first, last)
        probs = jnp.exp(scores - sums[:, :, first:last])
        probs_low = probs.astype(jnp.bfloat16)
        grad_block = grads[:, first:last]
        d_values = d_values.at[:, :last].add(jnp.einsum('shqk,sqhd->skhd', probs_low, grad_block, preferred_element_type=jnp.float32))
        d_probs = jnp.einsum('sqhd,skhd->shqk', grad_block, values[:, :last], preferred_element_type=jnp.float32)
        delta = lax.optimization_barrier(jnp.sum(probs * d_probs, axis=-1, keepdims=True))
        d_scores = (probs * (d_probs - delta) * scale).astype(jnp.bfloat16)
        d_queries.append(jnp.einsum('shqk,skhd->sqhd', d_scores, keys[:, :last], preferred_element_type=jnp.float32))
        d_keys = d_keys.at[:, :last].add(jnp.einsum('shqk,sqhd->skhd', d_scores, queries[:, first:last], preferred_element_type=jnp.float32))
    return (jnp.concatenate(d_queries, axis=1), d_keys, d_values)

def reference(inputs, w_query, w_key, w_value, q_gain, k_gain, w_out, attn_gain, w_gate, w_up, w_down, mlp_gain, cotangent):
    count = TOKENS // L
    cosine, sine = rope_tables(L, L, HD)
    gain_q = q_gain.astype(jnp.float32).reshape(D)
    gain_k = k_gain.astype(jnp.float32).reshape(D)
    gain_a = attn_gain.astype(jnp.float32)
    gain_m = mlp_gain.astype(jnp.float32)
    shape4 = (1, L, H, HD)

    def one_sequence(carry, pair):
        rows, upstream_low = pair
        query_raw = dot_plain(rows, w_query)
        key_raw = dot_plain(rows, w_key)
        value_low = dot_plain(rows, w_value).astype(jnp.bfloat16)
        rate_q = lax.rsqrt(lax.optimization_barrier(jnp.mean(query_raw * query_raw, axis=1, keepdims=True)) + epsilon)
        rate_k = lax.rsqrt(lax.optimization_barrier(jnp.mean(key_raw * key_raw, axis=1, keepdims=True)) + epsilon)
        hat_q = query_raw * rate_q
        hat_k = key_raw * rate_k
        query_rot = rotate((hat_q * gain_q).reshape(L, H, HD), cosine, sine, 1.0).astype(jnp.bfloat16).reshape(shape4)
        key_rot = rotate((hat_k * gain_k).reshape(L, H, HD), cosine, sine, 1.0).astype(jnp.bfloat16).reshape(shape4)
        value4 = value_low.reshape(shape4)
        attn_low, log_sums = attend(query_rot, key_rot, value4)
        attn_flat = attn_low.reshape(L, D)
        attn_proj = dot_plain(attn_flat, w_out)
        rate_a = lax.rsqrt(lax.optimization_barrier(jnp.mean(attn_proj * attn_proj, axis=1, keepdims=True)) + epsilon)
        hat_a = attn_proj * rate_a
        resid = rows.astype(jnp.float32) + hat_a * gain_a
        resid_low = resid.astype(jnp.bfloat16)
        gate = dot_plain(resid_low, w_gate)
        up_part = dot_plain(resid_low, w_up)
        sigma = jax.nn.sigmoid(gate)
        silu_gate = gate * sigma
        hidden = (silu_gate * up_part).astype(jnp.bfloat16)
        mlp_proj = dot_plain(hidden, w_down)
        rate_m = lax.rsqrt(lax.optimization_barrier(jnp.mean(mlp_proj * mlp_proj, axis=1, keepdims=True)) + epsilon)
        hat_m = mlp_proj * rate_m
        output = resid + hat_m * gain_m
        upstream = upstream_low.astype(jnp.float32)
        grad_gain_m = lax.optimization_barrier(jnp.sum(upstream * hat_m, axis=0))
        scaled_m = upstream * gain_m
        d_mlp = (rate_m * (scaled_m - hat_m * lax.optimization_barrier(jnp.mean(scaled_m * hat_m, axis=1, keepdims=True)))).astype(jnp.bfloat16)
        grad_down = dot_left_t(hidden, d_mlp)
        d_hidden = dot_right_t(d_mlp, w_down)
        d_gate = (d_hidden * up_part * sigma * (1.0 + gate * (1.0 - sigma))).astype(jnp.bfloat16)
        d_up = (d_hidden * silu_gate).astype(jnp.bfloat16)
        grad_gate = dot_left_t(resid_low, d_gate)
        grad_up = dot_left_t(resid_low, d_up)
        d_resid = upstream + dot_right_t(d_gate, w_gate) + dot_right_t(d_up, w_up)
        grad_gain_a = lax.optimization_barrier(jnp.sum(d_resid * hat_a, axis=0))
        scaled_a = d_resid * gain_a
        d_attn_proj = (rate_a * (scaled_a - hat_a * lax.optimization_barrier(jnp.mean(scaled_a * hat_a, axis=1, keepdims=True)))).astype(jnp.bfloat16)
        grad_out = dot_left_t(attn_flat, d_attn_proj)
        d_attn = dot_right_t(d_attn_proj, w_out).astype(jnp.bfloat16)
        d_qrot, d_krot, d_vals = attend_back(query_rot, key_rot, value4, log_sums, d_attn.reshape(shape4))
        d_qn = rotate(d_qrot.reshape(L, H, HD), cosine, sine, -1.0).reshape(L, D)
        d_kn = rotate(d_krot.reshape(L, H, HD), cosine, sine, -1.0).reshape(L, D)
        grad_gain_q = lax.optimization_barrier(jnp.sum(d_qn * hat_q, axis=0)).reshape(H, HD)
        grad_gain_k = lax.optimization_barrier(jnp.sum(d_kn * hat_k, axis=0)).reshape(H, HD)
        scaled_q = d_qn * gain_q
        scaled_k = d_kn * gain_k
        d_query = (rate_q * (scaled_q - hat_q * lax.optimization_barrier(jnp.mean(scaled_q * hat_q, axis=1, keepdims=True)))).astype(jnp.bfloat16)
        d_key = (rate_k * (scaled_k - hat_k * lax.optimization_barrier(jnp.mean(scaled_k * hat_k, axis=1, keepdims=True)))).astype(jnp.bfloat16)
        d_value = d_vals.reshape(L, D).astype(jnp.bfloat16)
        grad_query = dot_left_t(rows, d_query)
        grad_key = dot_left_t(rows, d_key)
        grad_value = dot_left_t(rows, d_value)
        input_grad = d_resid + dot_right_t(d_query, w_query) + dot_right_t(d_key, w_key) + dot_right_t(d_value, w_value)
        terms = (grad_query, grad_key, grad_value, grad_gain_q, grad_gain_k, grad_out, grad_gain_a, grad_gate, grad_up, grad_down, grad_gain_m)
        carry = tuple((held + term for held, term in zip(carry, terms)))
        return (carry, (output, input_grad))
    start = (jnp.zeros((D, D), jnp.float32), jnp.zeros((D, D), jnp.float32), jnp.zeros((D, D), jnp.float32), jnp.zeros((H, HD), jnp.float32), jnp.zeros((H, HD), jnp.float32), jnp.zeros((D, D), jnp.float32), jnp.zeros((D,), jnp.float32), jnp.zeros((D, FF), jnp.float32), jnp.zeros((D, FF), jnp.float32), jnp.zeros((FF, D), jnp.float32), jnp.zeros((D,), jnp.float32))
    totals, stacked = lax.scan(one_sequence, start, (inputs.reshape(count, L, D), cotangent.reshape(count, L, D)))
    output = stacked[0].reshape(TOKENS, D)
    input_grad = stacked[1].reshape(TOKENS, D)
    return (output, input_grad, totals[0], totals[1], totals[2], totals[3], totals[4], totals[5], totals[6], totals[7], totals[8], totals[9], totals[10])
```

```python
import functools

import jax
import jax.numpy as jnp
from jax import lax
from jax.experimental import pallas as pl
from jax.experimental.pallas import tpu as pltpu
from jax.sharding import PartitionSpec as P

HD = 128
L = 1024

epsilon = 1e-06
rope_base = 500000.0

BF = jnp.bfloat16
F32 = jnp.float32


def dot_plain(left, right):
    return jnp.dot(left, right, preferred_element_type=F32)


def dot_right_t(left, right):
    return lax.dot_general(left, right, (((1,), (1,)), ((), ())), preferred_element_type=F32)


def dot_left_t(left, right):
    return lax.dot_general(left, right, (((0,), (0,)), ((), ())), preferred_element_type=F32)


def rope_tables():
    half = HD // 2
    freqs = rope_base ** (-2.0 * jnp.arange(half, dtype=F32) / HD)
    angles = jnp.arange(L).astype(F32)[:, None] * freqs[None, :]
    cosine, sine = jnp.cos(angles), jnp.sin(angles)
    return (
        jnp.concatenate([cosine, cosine], axis=1),
        jnp.concatenate([-sine, sine], axis=1),
    )


def masked_scores(queries, keys, rows, last):
    scores = dot_right_t(queries, keys) * (HD ** (-0.5))
    row = lax.broadcasted_iota(jnp.int32, (rows, last), 0) + (last - rows)
    col = lax.broadcasted_iota(jnp.int32, (rows, last), 1)
    return jnp.where(col <= row, scores, -1e30)


def forward_kernel(n, rows, me_ref, *refs):
    q_in, k_in, v_in = refs[:n], refs[n : 2 * n], refs[2 * n : 3 * n]
    rate_q, rate_k, gain_q, gain_k, cosine, sine = refs[3 * n : 3 * n + 6]
    attn, q_out, k_out, v_out, lse = refs[3 * n + 6 :]
    me = me_ref[0]

    def place(s):
        return pl.multiple_of(lax.rem(me - s + n, n) * rows, rows)

    for s in range(n):
        at = pl.ds(place(s), rows)
        c, d = cosine[at, :], sine[at, :]
        for src, rate, gain, dst in (
            (q_in[s], rate_q, gain_q, q_out),
            (k_in[s], rate_k, gain_k, k_out),
        ):
            normed = src[...] * rate[at, :] * gain[0]
            turned = normed * c + pltpu.roll(normed, HD // 2, 1) * d
            dst[at, :] = turned.astype(BF)
        v_out[at, :] = v_in[s][...].astype(BF)
    for piece in range(n):
        first, last = piece * rows, (piece + 1) * rows
        scores = masked_scores(q_out[first:last, :], k_out[:last, :], rows, last)
        peak = jnp.max(scores, axis=1, keepdims=True)
        grown = jnp.exp(scores - peak)
        total = jnp.sum(grown, axis=1, keepdims=True)
        lse[0, first:last, :] = peak + jnp.log(total)
        probs = (grown * (1.0 / total)).astype(BF)
        attn[pl.ds(place(piece), rows), :] = dot_plain(probs, v_out[:last, :]).astype(BF)


def backward_kernel(n, rows, me_ref, *refs):
    q_in, k_in, g_in = refs[:n], refs[n : 2 * n], refs[2 * n : 3 * n]
    (rate_q, rate_k, gain_q, gain_k, cosine, sine, q_rot, k_rot, value, lse) = refs[
        3 * n : 3 * n + 10
    ]
    t_q, t_k, d_v, sums, gains = refs[3 * n + 10 : 3 * n + 15]
    grads, acc_q, acc_k, acc_v = refs[3 * n + 15 :]
    me = me_ref[0]
    scale = HD ** (-0.5)

    def place(s):
        return pl.multiple_of(lax.rem(me - s + n, n) * rows, rows)

    for s in range(n):
        grads[pl.ds(place(s), rows), :] = g_in[s][...]
    acc_k[...] = jnp.zeros_like(acc_k)
    acc_v[...] = jnp.zeros_like(acc_v)
    for piece in range(n):
        first, last = piece * rows, (piece + 1) * rows
        queries, keys = q_rot[first:last, :], k_rot[:last, :]
        grad = grads[first:last, :]
        scores = masked_scores(queries, keys, rows, last)
        probs = jnp.exp(scores - lse[0, first:last, :])
        d_probs = dot_right_t(grad, value[:last, :])
        delta = jnp.sum(probs * d_probs, axis=1, keepdims=True)
        d_scores = (probs * (d_probs - delta) * scale).astype(BF)
        acc_v[:last, :] += dot_left_t(probs.astype(BF), grad)
        acc_q[first:last, :] = dot_plain(d_scores, keys)
        acc_k[:last, :] += dot_left_t(d_scores, queries)
    ones = jnp.ones((8, HD), F32)
    head = pl.program_id(0)
    for which, (acc, src, rate, gain, out) in enumerate(
        ((acc_q, q_in, rate_q, gain_q, t_q), (acc_k, k_in, rate_k, gain_k, t_k))
    ):
        column = jnp.zeros((1, HD), F32)
        for s in range(n):
            at = pl.ds(place(s), rows)
            grad = acc[at, :]
            normed = grad * cosine[at, :] - pltpu.roll(grad, HD // 2, 1) * sine[at, :]
            hat = src[s][...] * rate[at, :]
            column = column + jnp.sum(normed * hat, axis=0, keepdims=True)
            scaled = normed * gain[0]
            out[s * rows : (s + 1) * rows, :] = scaled
            line = lax.dot_general(
                ones,
                scaled * hat,
                (((1,), (1,)), ((), ())),
                precision=lax.Precision.HIGHEST,
                preferred_element_type=F32,
            )
            here = (which, slice(None), slice(s * rows, (s + 1) * rows))

            @pl.when(head == 0)
            def _():
                sums[here] = line

            @pl.when(head > 0)
            def _():
                sums[here] += line

        gains[0, which : which + 1, :] = column
    for s in range(n):
        d_v[s * rows : (s + 1) * rows, :] = acc_v[pl.ds(place(s), rows), :].astype(BF)


def attention_forward(me, pieces, rate_q, rate_k, gain_q, gain_k, cosine, sine):
    n, rows = len(pieces), pieces[0].shape[0]
    heads = gain_q.shape[0]

    def part(offset):
        return [pl.BlockSpec((rows, HD), lambda h, m, o=offset: (0, o * heads + h))] * n

    whole = pl.BlockSpec((L, HD), lambda h, m: (0, 0))
    gain = pl.BlockSpec((1, 1, HD), lambda h, m: (h, 0, 0))
    column = pl.BlockSpec((L, HD), lambda h, m: (0, h))
    low = jax.ShapeDtypeStruct((L, heads * HD), BF)
    return pl.pallas_call(
        functools.partial(forward_kernel, n, rows),
        grid_spec=pltpu.PrefetchScalarGridSpec(
            num_scalar_prefetch=1,
            grid=(heads,),
            in_specs=part(0) + part(1) + part(2) + [whole, whole, gain, gain, whole, whole],
            out_specs=[column] * 4 + [pl.BlockSpec((1, L, 1), lambda h, m: (h, 0, 0))],
        ),
        out_shape=[low] * 4 + [jax.ShapeDtypeStruct((heads, L, 1), F32)],
        compiler_params=pltpu.CompilerParams(vmem_limit_bytes=48 << 20),
        cost_estimate=pl.CostEstimate(
            flops=2 * heads * L * L * HD,
            bytes_accessed=12 * heads * L * HD + 10 * heads * L * HD,
            transcendentals=heads * L * L // 2,
        ),
        name="attention_forward",
    )(
        me,
        *pieces,
        *pieces,
        *pieces,
        rate_q,
        rate_k,
        gain_q[:, None, :],
        gain_k[:, None, :],
        cosine,
        sine,
    )


def attention_backward(
    me, pieces, grads, rate_q, rate_k, gain_q, gain_k, cosine, sine, q_rot, k_rot, value, lse
):
    n, rows = len(pieces), pieces[0].shape[0]
    heads = gain_q.shape[0]

    def part(offset):
        return [pl.BlockSpec((rows, HD), lambda h, m, o=offset: (0, o * heads + h))] * n

    whole = pl.BlockSpec((L, HD), lambda h, m: (0, 0))
    gain = pl.BlockSpec((1, 1, HD), lambda h, m: (h, 0, 0))
    column = pl.BlockSpec((L, HD), lambda h, m: (0, h))
    wide = jax.ShapeDtypeStruct((L, heads * HD), F32)
    return pl.pallas_call(
        functools.partial(backward_kernel, n, rows),
        grid_spec=pltpu.PrefetchScalarGridSpec(
            num_scalar_prefetch=1,
            grid=(heads,),
            in_specs=part(0)
            + part(1)
            + part(0)
            + [whole, whole, gain, gain, whole, whole]
            + [column] * 3
            + [pl.BlockSpec((1, L, 1), lambda h, m: (h, 0, 0))],
            out_specs=[column] * 3
            + [
                pl.BlockSpec((2, 8, L), lambda h, m: (0, 0, 0)),
                pl.BlockSpec((1, 2, HD), lambda h, m: (h, 0, 0)),
            ],
            scratch_shapes=[
                pltpu.VMEM((L, HD), BF),
                pltpu.VMEM((L, HD), F32),
                pltpu.VMEM((L, HD), F32),
                pltpu.VMEM((L, HD), F32),
            ],
        ),
        out_shape=[
            wide,
            wide,
            jax.ShapeDtypeStruct((L, heads * HD), BF),
            jax.ShapeDtypeStruct((2, 8, L), F32),
            jax.ShapeDtypeStruct((heads, 2, HD), F32),
        ],
        compiler_params=pltpu.CompilerParams(vmem_limit_bytes=48 << 20),
        cost_estimate=pl.CostEstimate(
            flops=5 * heads * L * L * HD,
            bytes_accessed=26 * heads * L * HD,
            transcendentals=heads * L * L // 2,
        ),
        name="attention_backward",
    )(
        me,
        *pieces,
        *pieces,
        *grads,
        rate_q,
        rate_k,
        gain_q[:, None, :],
        gain_k[:, None, :],
        cosine,
        sine,
        q_rot,
        k_rot,
        value,
        lse,
    )


def local(
    n,
    groups,
    inputs,
    w_query,
    w_key,
    w_value,
    q_gain,
    k_gain,
    w_out,
    attn_gain,
    w_gate,
    w_up,
    w_down,
    mlp_gain,
    cotangent,
):
    rows, width = inputs.shape
    heads, slice_q = q_gain.shape
    head_cols = heads * HD
    units = w_gate.shape[1]
    me = lax.axis_index("mp").astype(jnp.int32)
    me_ref = me.reshape(1)
    ring = [(i, (i + 1) % n) for i in range(n)]

    def shift(value):
        return lax.ppermute(value, "mp", ring)

    def reorder(stacked):
        turned = stacked[::-1]
        return lax.dynamic_slice_in_dim(
            jnp.concatenate([turned, turned], axis=0), n - 1 - me, n, axis=0
        )

    def gather_ring(own):
        held = [own]
        for _ in range(n - 1):
            held.append(shift(held[-1]))
        return held

    def scatter_ring(partial_of):
        running = None
        for s in range(1, n):
            term = partial_of(s)
            if running is not None:
                term = term + running.astype(F32)
            running = shift(term.astype(BF))
        return partial_of(0) + running.astype(F32)

    w_qkv = lax.all_gather(
        jnp.concatenate([w_query, w_key, w_value], axis=1), "dp", axis=0, tiled=True
    )
    small = jnp.concatenate(
        [q_gain.reshape(-1), k_gain.reshape(-1), attn_gain, mlp_gain], axis=0
    )
    small = lax.all_gather(small, "dp", axis=0, tiled=False).astype(F32)
    count = heads * slice_q
    gain_q = small[:, :count].reshape(groups, heads, slice_q).transpose(1, 0, 2).reshape(heads, HD)
    gain_k = (
        small[:, count : 2 * count]
        .reshape(groups, heads, slice_q)
        .transpose(1, 0, 2)
        .reshape(heads, HD)
    )
    own_cols = attn_gain.shape[0]
    gain_a = small[:, 2 * count : 2 * count + own_cols].reshape(width)
    gain_m = small[:, 2 * count + own_cols :].reshape(width)
    full_out = lax.all_gather(w_out, "dp", axis=1, tiled=True)
    full_gate = lax.all_gather(w_gate, "dp", axis=0, tiled=True)
    full_up = lax.all_gather(w_up, "dp", axis=0, tiled=True)
    full_down = lax.all_gather(w_down, "dp", axis=1, tiled=True)
    cosine, sine = rope_tables()

    held_x = gather_ring(inputs)
    pieces = [dot_plain(x, w_qkv) for x in held_x]
    squares = jnp.stack(
        [
            jnp.stack(
                [
                    jnp.sum(jnp.square(p[:, :head_cols]), axis=1),
                    jnp.sum(jnp.square(p[:, head_cols : 2 * head_cols]), axis=1),
                ]
            )
            for p in pieces
        ]
    )
    squares = lax.psum(reorder(squares), "mp")
    rates = lax.rsqrt(squares / width + epsilon)
    rate_q = jnp.broadcast_to(rates[:, 0].reshape(L, 1), (L, HD))
    rate_k = jnp.broadcast_to(rates[:, 1].reshape(L, 1), (L, HD))
    attn, q_rot, k_rot, value, lse = attention_forward(
        me_ref, pieces, rate_q, rate_k, gain_q, gain_k, cosine, sine
    )
    attn_proj = scatter_ring(
        lambda s: dot_plain(attn[s * rows : (s + 1) * rows], full_out)
    )
    rate_a = lax.rsqrt(jnp.mean(attn_proj * attn_proj, axis=1, keepdims=True) + epsilon)
    hat_a = attn_proj * rate_a
    resid = inputs.astype(F32) + hat_a * gain_a
    resid_low = resid.astype(BF)

    held_r = gather_ring(resid_low)
    gates, ups, hiddens = [], [], []
    for r in held_r:
        gate = dot_plain(r, full_gate)
        up = dot_plain(r, full_up)
        gates.append(gate)
        ups.append(up)
        hiddens.append((gate * jax.nn.sigmoid(gate) * up).astype(BF))
    mlp_proj = scatter_ring(lambda s: dot_plain(hiddens[s], full_down))
    rate_m = lax.rsqrt(jnp.mean(mlp_proj * mlp_proj, axis=1, keepdims=True) + epsilon)
    hat_m = mlp_proj * rate_m
    output = resid + hat_m * gain_m

    upstream = cotangent.astype(F32)
    grad_gain_m = jnp.sum(upstream * hat_m, axis=0)
    scaled_m = upstream * gain_m
    d_mlp = (
        rate_m * (scaled_m - hat_m * jnp.mean(scaled_m * hat_m, axis=1, keepdims=True))
    ).astype(BF)
    held_m = gather_ring(d_mlp)
    d_gates, d_ups = [], []
    for s in range(n):
        gate, up = gates[s], ups[s]
        sigma = jax.nn.sigmoid(gate)
        d_hidden = dot_right_t(held_m[s], full_down)
        d_gates.append((d_hidden * up * sigma * (1.0 + gate * (1.0 - sigma))).astype(BF))
        d_ups.append((d_hidden * (gate * sigma)).astype(BF))
    d_resid = cotangent.astype(F32) + scatter_ring(
        lambda s: dot_right_t(d_gates[s], full_gate) + dot_right_t(d_ups[s], full_up)
    )
    all_r = jnp.concatenate(held_r, axis=0)
    d_gate_up = jnp.concatenate(
        [jnp.concatenate(d_gates, axis=0), jnp.concatenate(d_ups, axis=0)], axis=1
    )
    grad_down = lax.psum_scatter(
        dot_left_t(jnp.concatenate(hiddens, axis=0), jnp.concatenate(held_m, axis=0)).astype(BF),
        "dp",
        scatter_dimension=1,
        tiled=True,
    ).astype(F32)
    grad_gate_up = lax.psum_scatter(
        dot_left_t(all_r, d_gate_up).astype(BF), "dp", scatter_dimension=0, tiled=True
    )
    grad_gate = grad_gate_up[:, :units].astype(F32)
    grad_up = grad_gate_up[:, units:].astype(F32)

    grad_gain_a = jnp.sum(d_resid * hat_a, axis=0)
    scaled_a = d_resid * gain_a
    d_attn_proj = (
        rate_a * (scaled_a - hat_a * jnp.mean(scaled_a * hat_a, axis=1, keepdims=True))
    ).astype(BF)
    held_a = gather_ring(d_attn_proj)
    d_attn = [dot_right_t(a, full_out).astype(BF) for a in held_a]
    grad_out = lax.psum_scatter(
        dot_left_t(attn, jnp.concatenate(held_a, axis=0)).astype(BF),
        "dp",
        scatter_dimension=1,
        tiled=True,
    ).astype(F32)
    t_q, t_k, d_value, sums, head_gains = attention_backward(
        me_ref,
        pieces,
        d_attn,
        rate_q,
        rate_k,
        gain_q,
        gain_k,
        cosine,
        sine,
        q_rot,
        k_rot,
        value,
        lse,
    )
    sums = reorder(sums[:, 0, :].reshape(2, n, rows).transpose(1, 0, 2))
    sums = lax.psum(sums, "mp")
    back = reorder(jnp.concatenate([rates, sums / width], axis=1))
    d_qkv = []
    for s in range(n):
        at = slice(s * rows, (s + 1) * rows)
        parts = []
        for which, t in enumerate((t_q, t_k)):
            rate = back[s, which][:, None]
            raw = pieces[s][:, which * head_cols : (which + 1) * head_cols]
            parts.append((rate * (t[at] - raw * (rate * back[s, 2 + which][:, None]))).astype(BF))
        parts.append(d_value[at])
        d_qkv.append(jnp.concatenate(parts, axis=1))
    grad_qkv = lax.psum_scatter(
        dot_left_t(jnp.concatenate(held_x, axis=0), jnp.concatenate(d_qkv, axis=0)).astype(BF),
        "dp",
        scatter_dimension=0,
        tiled=True,
    )
    grad_query = grad_qkv[:, :head_cols].astype(F32)
    grad_key = grad_qkv[:, head_cols : 2 * head_cols].astype(F32)
    grad_value = grad_qkv[:, 2 * head_cols :].astype(F32)
    input_grad = d_resid + scatter_ring(lambda s: dot_right_t(d_qkv[s], w_qkv))

    post = lax.psum(jnp.stack([grad_gain_a, grad_gain_m]), "mp")
    post = post.reshape(2, groups, own_cols).transpose(1, 0, 2).reshape(groups, 2 * own_cols)
    own = head_gains.transpose(1, 0, 2).reshape(2, heads, groups, slice_q)
    own = own.transpose(2, 0, 1, 3).reshape(groups, 2 * count)
    totals = lax.psum(jnp.concatenate([own, post], axis=1), "dp")
    mine = lax.dynamic_index_in_dim(totals, lax.axis_index("dp"), 0, keepdims=False)
    return (
        output,
        input_grad,
        grad_query,
        grad_key,
        grad_value,
        mine[:count].reshape(heads, slice_q),
        mine[count : 2 * count].reshape(heads, slice_q),
        grad_out,
        mine[2 * count : 2 * count + own_cols],
        grad_gate,
        grad_up,
        grad_down,
        mine[2 * count + own_cols :],
    )


def solution(mesh):
    in_specs = (
        P(("dp", "mp"), None),
        P("dp", "mp"),
        P("dp", "mp"),
        P("dp", "mp"),
        P("mp", "dp"),
        P("mp", "dp"),
        P("mp", "dp"),
        P("dp"),
        P("dp", "mp"),
        P("dp", "mp"),
        P("mp", "dp"),
        P("dp"),
        P(("dp", "mp"), None),
    )
    out_specs = (
        P(("dp", "mp"), None),
        P(("dp", "mp"), None),
        P("dp", "mp"),
        P("dp", "mp"),
        P("dp", "mp"),
        P("mp", "dp"),
        P("mp", "dp"),
        P("mp", "dp"),
        P("dp"),
        P("dp", "mp"),
        P("dp", "mp"),
        P("mp", "dp"),
        P("dp"),
    )
    body = functools.partial(local, mesh.shape["mp"], mesh.shape["dp"])
    return jax.shard_map(body, mesh=mesh, in_specs=in_specs, out_specs=out_specs, check_vma=False)
```

```python
import functools

import jax
import jax.numpy as jnp
from jax import lax
from jax.experimental import pallas as pl
from jax.experimental.layout import Layout, with_layout_constraint
from jax.experimental.pallas import tpu as pltpu
from jax.sharding import PartitionSpec as P


HD = 128
L = 1024

epsilon = 1e-06
rope_base = 500000.0

BF = jnp.bfloat16
F32 = jnp.float32


def dot_plain(left, right):
    return jnp.dot(left, right, preferred_element_type=F32)


def dot_right_t(left, right):
    return lax.dot_general(left, right, (((1,), (1,)), ((), ())), preferred_element_type=F32)


def dot_left_t(left, right):
    return lax.dot_general(left, right, (((0,), (0,)), ((), ())), preferred_element_type=F32)


def row_major(value):
    return with_layout_constraint(value, Layout(major_to_minor=(0, 1)))


def rope_tables():
    half = HD // 2
    freqs = rope_base ** (-2.0 * jnp.arange(half, dtype=F32) / HD)
    angles = jnp.arange(L).astype(F32)[:, None] * freqs[None, :]
    cosine, sine = jnp.cos(angles), jnp.sin(angles)
    return (
        jnp.concatenate([cosine, cosine], axis=1),
        jnp.concatenate([-sine, sine], axis=1),
    )


def masked_scores(queries, keys, rows, last):
    scores = dot_right_t(queries, keys) * (HD ** (-0.5))
    row = lax.broadcasted_iota(jnp.int32, (rows, last), 0) + (last - rows)
    col = lax.broadcasted_iota(jnp.int32, (rows, last), 1)
    return jnp.where(col <= row, scores, -1e30)


def forward_kernel(n, rows, me_ref, *refs):
    q_in, k_in, v_in = refs[:n], refs[n : 2 * n], refs[2 * n : 3 * n]
    rate_q, rate_k, gain_q, gain_k, cosine, sine = refs[3 * n : 3 * n + 6]
    attn, q_out, k_out, v_out, lse = refs[3 * n + 6 :]
    me = me_ref[0]

    def place(s):
        return pl.multiple_of(lax.rem(me - s + n, n) * rows, rows)

    for s in range(n):
        at = pl.ds(place(s), rows)
        c, d = cosine[at, :], sine[at, :]
        for src, rate, gain, dst in (
            (q_in[s], rate_q, gain_q, q_out),
            (k_in[s], rate_k, gain_k, k_out),
        ):
            normed = src[...] * rate[at, :] * gain[0]
            turned = normed * c + pltpu.roll(normed, HD // 2, 1) * d
            dst[at, :] = turned.astype(BF)
        v_out[at, :] = v_in[s][...].astype(BF)
    for piece in range(n):
        first, last = piece * rows, (piece + 1) * rows
        scores = masked_scores(q_out[first:last, :], k_out[:last, :], rows, last)
        peak = jnp.max(scores, axis=1, keepdims=True)
        grown = jnp.exp(scores - peak)
        total = jnp.sum(grown, axis=1, keepdims=True)
        lse[0, first:last, :] = peak + jnp.log(total)
        probs = (grown * (1.0 / total)).astype(BF)
        attn[pl.ds(place(piece), rows), :] = dot_plain(probs, v_out[:last, :]).astype(BF)


def backward_kernel(n, rows, me_ref, *refs):
    q_in, k_in, g_in = refs[:n], refs[n : 2 * n], refs[2 * n : 3 * n]
    (rate_q, rate_k, gain_q, gain_k, cosine, sine, q_rot, k_rot, value, lse) = refs[
        3 * n : 3 * n + 10
    ]
    t_q, t_k, d_v, sums, gains = refs[3 * n + 10 : 3 * n + 15]
    grads, acc_q, acc_k, acc_v = refs[3 * n + 15 :]
    me = me_ref[0]
    scale = HD ** (-0.5)

    def place(s):
        return pl.multiple_of(lax.rem(me - s + n, n) * rows, rows)

    for s in range(n):
        grads[pl.ds(place(s), rows), :] = g_in[s][...]
    acc_k[...] = jnp.zeros_like(acc_k)
    acc_v[...] = jnp.zeros_like(acc_v)
    for piece in range(n):
        first, last = piece * rows, (piece + 1) * rows
        queries, keys = q_rot[first:last, :], k_rot[:last, :]
        grad = grads[first:last, :]
        scores = masked_scores(queries, keys, rows, last)
        probs = jnp.exp(scores - lse[0, first:last, :])
        d_probs = dot_right_t(grad, value[:last, :])
        delta = jnp.sum(probs * d_probs, axis=1, keepdims=True)
        d_scores = (probs * (d_probs - delta) * scale).astype(BF)
        acc_v[:last, :] += dot_left_t(probs.astype(BF), grad)
        acc_q[first:last, :] = dot_plain(d_scores, keys)
        acc_k[:last, :] += dot_left_t(d_scores, queries)
    ones = jnp.ones((8, HD), F32)
    head = pl.program_id(0)
    for which, (acc, src, rate, gain, out) in enumerate(
        ((acc_q, q_in, rate_q, gain_q, t_q), (acc_k, k_in, rate_k, gain_k, t_k))
    ):
        column = jnp.zeros((1, HD), F32)
        for s in range(n):
            at = pl.ds(place(s), rows)
            grad = acc[at, :]
            normed = grad * cosine[at, :] - pltpu.roll(grad, HD // 2, 1) * sine[at, :]
            hat = src[s][...] * rate[at, :]
            column = column + jnp.sum(normed * hat, axis=0, keepdims=True)
            scaled = normed * gain[0]
            out[s * rows : (s + 1) * rows, :] = scaled
            line = lax.dot_general(
                ones,
                scaled * hat,
                (((1,), (1,)), ((), ())),
                precision=lax.Precision.HIGHEST,
                preferred_element_type=F32,
            )
            here = (which, slice(None), slice(s * rows, (s + 1) * rows))

            @pl.when(head == 0)
            def _():
                sums[here] = line

            @pl.when(head > 0)
            def _():
                sums[here] += line

        gains[0, which : which + 1, :] = column
    for s in range(n):
        d_v[s * rows : (s + 1) * rows, :] = acc_v[pl.ds(place(s), rows), :].astype(BF)


def attention_forward(me, pieces, rate_q, rate_k, gain_q, gain_k, cosine, sine):
    n, rows = len(pieces), pieces[0].shape[0]
    heads = gain_q.shape[0]

    def part(offset):
        return [pl.BlockSpec((rows, HD), lambda h, m, o=offset: (0, o * heads + h))] * n

    whole = pl.BlockSpec((L, HD), lambda h, m: (0, 0))
    gain = pl.BlockSpec((1, 1, HD), lambda h, m: (h, 0, 0))
    column = pl.BlockSpec((L, HD), lambda h, m: (0, h))
    low = jax.ShapeDtypeStruct((L, heads * HD), BF)
    return pl.pallas_call(
        functools.partial(forward_kernel, n, rows),
        grid_spec=pltpu.PrefetchScalarGridSpec(
            num_scalar_prefetch=1,
            grid=(heads,),
            in_specs=part(0) + part(1) + part(2) + [whole, whole, gain, gain, whole, whole],
            out_specs=[column] * 4 + [pl.BlockSpec((1, L, 1), lambda h, m: (h, 0, 0))],
        ),
        out_shape=[low] * 4 + [jax.ShapeDtypeStruct((heads, L, 1), F32)],
        compiler_params=pltpu.CompilerParams(vmem_limit_bytes=48 << 20),
        cost_estimate=pl.CostEstimate(
            flops=2 * heads * L * L * HD,
            bytes_accessed=12 * heads * L * HD + 10 * heads * L * HD,
            transcendentals=heads * L * L // 2,
        ),
        name="attention_forward",
    )(
        me,
        *pieces,
        *pieces,
        *pieces,
        rate_q,
        rate_k,
        gain_q[:, None, :],
        gain_k[:, None, :],
        cosine,
        sine,
    )


def attention_backward(
    me, pieces, grads, rate_q, rate_k, gain_q, gain_k, cosine, sine, q_rot, k_rot, value, lse
):
    n, rows = len(pieces), pieces[0].shape[0]
    heads = gain_q.shape[0]

    def part(offset):
        return [pl.BlockSpec((rows, HD), lambda h, m, o=offset: (0, o * heads + h))] * n

    whole = pl.BlockSpec((L, HD), lambda h, m: (0, 0))
    gain = pl.BlockSpec((1, 1, HD), lambda h, m: (h, 0, 0))
    column = pl.BlockSpec((L, HD), lambda h, m: (0, h))
    wide = jax.ShapeDtypeStruct((L, heads * HD), F32)
    return pl.pallas_call(
        functools.partial(backward_kernel, n, rows),
        grid_spec=pltpu.PrefetchScalarGridSpec(
            num_scalar_prefetch=1,
            grid=(heads,),
            in_specs=part(0)
            + part(1)
            + part(0)
            + [whole, whole, gain, gain, whole, whole]
            + [column] * 3
            + [pl.BlockSpec((1, L, 1), lambda h, m: (h, 0, 0))],
            out_specs=[column] * 3
            + [
                pl.BlockSpec((2, 8, L), lambda h, m: (0, 0, 0)),
                pl.BlockSpec((1, 2, HD), lambda h, m: (h, 0, 0)),
            ],
            scratch_shapes=[
                pltpu.VMEM((L, HD), BF),
                pltpu.VMEM((L, HD), F32),
                pltpu.VMEM((L, HD), F32),
                pltpu.VMEM((L, HD), F32),
            ],
        ),
        out_shape=[
            wide,
            wide,
            jax.ShapeDtypeStruct((L, heads * HD), BF),
            jax.ShapeDtypeStruct((2, 8, L), F32),
            jax.ShapeDtypeStruct((heads, 2, HD), F32),
        ],
        compiler_params=pltpu.CompilerParams(vmem_limit_bytes=48 << 20),
        cost_estimate=pl.CostEstimate(
            flops=5 * heads * L * L * HD,
            bytes_accessed=26 * heads * L * HD,
            transcendentals=heads * L * L // 2,
        ),
        name="attention_backward",
    )(
        me,
        *pieces,
        *pieces,
        *grads,
        rate_q,
        rate_k,
        gain_q[:, None, :],
        gain_k[:, None, :],
        cosine,
        sine,
        q_rot,
        k_rot,
        value,
        lse,
    )


def local(
    n,
    groups,
    inputs,
    w_query,
    w_key,
    w_value,
    q_gain,
    k_gain,
    w_out,
    attn_gain,
    w_gate,
    w_up,
    w_down,
    mlp_gain,
    cotangent,
):
    rows, width = inputs.shape
    heads, slice_q = q_gain.shape
    head_cols = heads * HD
    units = w_gate.shape[1]
    me = lax.axis_index("mp").astype(jnp.int32)
    me_ref = me.reshape(1)
    ring = [(i, (i + 1) % n) for i in range(n)]

    def shift(value):
        return lax.ppermute(value, "mp", ring)

    def reorder(stacked):
        turned = stacked[::-1]
        return lax.dynamic_slice_in_dim(
            jnp.concatenate([turned, turned], axis=0), n - 1 - me, n, axis=0
        )

    def gather_ring(own, first=1, last=n - 1, after={}):
        held = [own]
        for s in range(first, last + 1):
            sent = held[-1]
            if s in after:
                sent = lax.optimization_barrier((sent, after[s]))[0]
            held.append(shift(sent))
        return held

    def scatter_ring(partial_of, after={}):
        running = None
        for s in range(1, n):
            term = partial_of(s)
            if running is not None:
                term = term + running.astype(F32)
            term = term.astype(BF)
            if s in after:
                term = lax.optimization_barrier((term, after[s]))[0]
            running = shift(term)
        return partial_of(0) + running.astype(F32)

    w_attn = lax.all_gather(
        row_major(jnp.concatenate([w_query, w_key, w_value, row_major(w_out.T)], axis=1)),
        "dp",
        axis=0,
        tiled=True,
    )
    w_qkv = w_attn[:, : 3 * head_cols]
    out_t = w_attn[:, 3 * head_cols :]
    small = jnp.concatenate(
        [q_gain.reshape(-1), k_gain.reshape(-1), attn_gain, mlp_gain], axis=0
    )
    small = lax.all_gather(small, "dp", axis=0, tiled=False).astype(F32)
    count = heads * slice_q
    gain_q = small[:, :count].reshape(groups, heads, slice_q).transpose(1, 0, 2).reshape(heads, HD)
    gain_k = (
        small[:, count : 2 * count]
        .reshape(groups, heads, slice_q)
        .transpose(1, 0, 2)
        .reshape(heads, HD)
    )
    own_cols = attn_gain.shape[0]
    gain_a = small[:, 2 * count : 2 * count + own_cols].reshape(width)
    gain_m = small[:, 2 * count + own_cols :].reshape(width)
    full_gate = lax.all_gather(w_gate, "dp", axis=0, tiled=True)
    full_up = lax.all_gather(w_up, "dp", axis=0, tiled=True)
    full_down = lax.all_gather(w_down, "dp", axis=1, tiled=True)
    cosine, sine = rope_tables()

    held_x = gather_ring(inputs, 1, n - 2)
    pieces = [dot_plain(x, w_qkv) for x in held_x]
    last, pieces[0] = lax.optimization_barrier((held_x[-1], pieces[0]))
    held_x.append(gather_ring(last, n - 1)[1])
    pieces.append(dot_plain(held_x[-1], w_qkv))
    squares = jnp.stack(
        [
            jnp.stack(
                [
                    jnp.sum(jnp.square(p[:, :head_cols]), axis=1),
                    jnp.sum(jnp.square(p[:, head_cols : 2 * head_cols]), axis=1),
                ]
            )
            for p in pieces
        ]
    )
    squares = lax.psum(reorder(squares), "mp")
    rates = lax.rsqrt(squares / width + epsilon)
    rate_q = jnp.broadcast_to(rates[:, 0].reshape(L, 1), (L, HD))
    rate_k = jnp.broadcast_to(rates[:, 1].reshape(L, 1), (L, HD))
    attn, q_rot, k_rot, value, lse = attention_forward(
        me_ref, pieces, rate_q, rate_k, gain_q, gain_k, cosine, sine
    )
    attn_proj = scatter_ring(lambda s: dot_right_t(attn[s * rows : (s + 1) * rows], out_t))
    rate_a = lax.rsqrt(jnp.mean(attn_proj * attn_proj, axis=1, keepdims=True) + epsilon)
    hat_a = attn_proj * rate_a
    resid = inputs.astype(F32) + hat_a * gain_a
    resid_low = resid.astype(BF)

    held_r = gather_ring(resid_low)
    gates, ups, hiddens = [], [], []
    for r in held_r:
        gate = dot_plain(r, full_gate)
        up = dot_plain(r, full_up)
        gates.append(gate)
        ups.append(up)
        hiddens.append((gate * jax.nn.sigmoid(gate) * up).astype(BF))
    mlp_proj = scatter_ring(lambda s: dot_plain(hiddens[s], full_down))
    rate_m = lax.rsqrt(jnp.mean(mlp_proj * mlp_proj, axis=1, keepdims=True) + epsilon)
    hat_m = mlp_proj * rate_m
    output = resid + hat_m * gain_m

    upstream = cotangent.astype(F32)
    grad_gain_m = jnp.sum(upstream * hat_m, axis=0)
    scaled_m = upstream * gain_m
    d_mlp = (
        rate_m * (scaled_m - hat_m * jnp.mean(scaled_m * hat_m, axis=1, keepdims=True))
    ).astype(BF)
    held_m = gather_ring(d_mlp)
    d_gates, d_ups = [], []
    for s in range(n):
        gate, up = gates[s], ups[s]
        sigma = jax.nn.sigmoid(gate)
        d_hidden = dot_right_t(held_m[s], full_down)
        d_gates.append((d_hidden * up * sigma * (1.0 + gate * (1.0 - sigma))).astype(BF))
        d_ups.append((d_hidden * (gate * sigma)).astype(BF))
    down = dot_left_t(jnp.concatenate(hiddens, axis=0), jnp.concatenate(held_m, axis=0)).astype(BF)
    d_resid = upstream + scatter_ring(
        lambda s: dot_right_t(d_gates[s], full_gate) + dot_right_t(d_ups[s], full_up),
        {1: held_m[-1]},
    )
    grad_down = lax.psum_scatter(down, "dp", scatter_dimension=1, tiled=True)
    d_gate_up = jnp.concatenate(
        [jnp.concatenate(d_gates, axis=0), jnp.concatenate(d_ups, axis=0)], axis=1
    )
    all_r = jnp.concatenate(held_r, axis=0)
    gate_up = dot_left_t(all_r, d_gate_up).astype(BF)

    grad_gain_a = jnp.sum(d_resid * hat_a, axis=0)
    scaled_a = d_resid * gain_a
    d_attn_proj = (
        rate_a * (scaled_a - hat_a * jnp.mean(scaled_a * hat_a, axis=1, keepdims=True))
    ).astype(BF)
    held_a = gather_ring(d_attn_proj, after={n - 1: grad_down})
    grad_gate_up = lax.psum_scatter(gate_up, "dp", scatter_dimension=0, tiled=True)
    d_attn = [dot_plain(a, out_t).astype(BF) for a in held_a]
    t_q, t_k, d_value, sums, head_gains = attention_backward(
        me_ref,
        pieces,
        d_attn,
        rate_q,
        rate_k,
        gain_q,
        gain_k,
        cosine,
        sine,
        q_rot,
        k_rot,
        value,
        lse,
    )
    sums = reorder(sums[:, 0, :].reshape(2, n, rows).transpose(1, 0, 2))
    sums = lax.psum(sums, "mp")
    back = reorder(jnp.concatenate([rates, sums / width], axis=1))
    d_qkv = []
    for s in range(n):
        at = slice(s * rows, (s + 1) * rows)
        parts = []
        for which, t in enumerate((t_q, t_k)):
            rate = back[s, which][:, None]
            raw = pieces[s][:, which * head_cols : (which + 1) * head_cols]
            parts.append((rate * (t[at] - raw * (rate * back[s, 2 + which][:, None]))).astype(BF))
        parts.append(d_value[at])
        d_qkv.append(jnp.concatenate(parts, axis=1))
    all_x, all_d = jnp.concatenate(held_x, axis=0), jnp.concatenate(d_qkv, axis=0)
    dw_qkv = dot_left_t(all_x, all_d).astype(BF)
    all_a = jnp.concatenate(held_a, axis=0)
    dw_out = dot_left_t(all_a, attn).astype(BF)
    grad_attn = lax.psum_scatter(
        jnp.concatenate([dw_qkv, dw_out], axis=1), "dp", scatter_dimension=0, tiled=True
    )
    grad_query = grad_attn[:, :head_cols].astype(F32)
    grad_key = grad_attn[:, head_cols : 2 * head_cols].astype(F32)
    grad_value = grad_attn[:, 2 * head_cols : 3 * head_cols].astype(F32)
    grad_out = grad_attn[:, 3 * head_cols :].astype(F32).T
    input_grad = d_resid + scatter_ring(
        lambda s: dot_right_t(d_qkv[s], w_qkv), {n - 1: grad_gate_up}
    )

    grad_gate = grad_gate_up[:, :units].astype(F32)
    grad_up = grad_gate_up[:, units:].astype(F32)

    post = lax.psum(jnp.stack([grad_gain_a, grad_gain_m]), "mp")
    post = post.reshape(2, groups, own_cols).transpose(1, 0, 2).reshape(groups, 2 * own_cols)
    own = head_gains.transpose(1, 0, 2).reshape(2, heads, groups, slice_q)
    own = own.transpose(2, 0, 1, 3).reshape(groups, 2 * count)
    totals = lax.psum(jnp.concatenate([own, post], axis=1), "dp")
    mine = lax.dynamic_index_in_dim(totals, lax.axis_index("dp"), 0, keepdims=False)
    return (
        output,
        input_grad,
        grad_query,
        grad_key,
        grad_value,
        mine[:count].reshape(heads, slice_q),
        mine[count : 2 * count].reshape(heads, slice_q),
        grad_out,
        mine[2 * count : 2 * count + own_cols],
        grad_gate,
        grad_up,
        grad_down.astype(F32),
        mine[2 * count + own_cols :],
    )


def solution(mesh):
    in_specs = (
        P(("dp", "mp"), None),
        P("dp", "mp"),
        P("dp", "mp"),
        P("dp", "mp"),
        P("mp", "dp"),
        P("mp", "dp"),
        P("mp", "dp"),
        P("dp"),
        P("dp", "mp"),
        P("dp", "mp"),
        P("mp", "dp"),
        P("dp"),
        P(("dp", "mp"), None),
    )
    out_specs = (
        P(("dp", "mp"), None),
        P(("dp", "mp"), None),
        P("dp", "mp"),
        P("dp", "mp"),
        P("dp", "mp"),
        P("mp", "dp"),
        P("mp", "dp"),
        P("mp", "dp"),
        P("dp"),
        P("dp", "mp"),
        P("dp", "mp"),
        P("mp", "dp"),
        P("dp"),
    )

    def body(*args):
        return local(mesh.shape["mp"], mesh.shape["dp"], *args)

    return jax.shard_map(body, mesh=mesh, in_specs=in_specs, out_specs=out_specs, check_vma=False)
```

```python
import functools

import jax
import jax.numpy as jnp
from jax import lax
from jax.experimental import pallas as pl
from jax.experimental.layout import Layout, with_layout_constraint
from jax.experimental.pallas import tpu as pltpu
from jax.sharding import PartitionSpec as P


HD = 128
L = 1024

epsilon = 1e-06
rope_base = 500000.0

BF = jnp.bfloat16
F32 = jnp.float32


def dot_plain(left, right):
    return jnp.dot(left, right, preferred_element_type=F32)


def dot_right_t(left, right):
    return lax.dot_general(left, right, (((1,), (1,)), ((), ())), preferred_element_type=F32)


def dot_left_t(left, right):
    return lax.dot_general(left, right, (((0,), (0,)), ((), ())), preferred_element_type=F32)


def row_major(value):
    return with_layout_constraint(value, Layout(major_to_minor=(0, 1)))


def rope_tables():
    half = HD // 2
    freqs = rope_base ** (-2.0 * jnp.arange(half, dtype=F32) / HD)
    angles = jnp.arange(L).astype(F32)[:, None] * freqs[None, :]
    cosine, sine = jnp.cos(angles), jnp.sin(angles)
    return (
        jnp.concatenate([cosine, cosine], axis=1),
        jnp.concatenate([-sine, sine], axis=1),
    )


def masked_scores(keys, queries, last, rows):
    scores = dot_right_t(keys, queries) * (HD ** (-0.5))
    row = lax.broadcasted_iota(jnp.int32, (rows, rows), 0)
    col = lax.broadcasted_iota(jnp.int32, (rows, rows), 1)
    corner = jnp.where(row <= col, scores[last - rows :, :], -1e30)
    if last == rows:
        return corner
    return jnp.concatenate([scores[: last - rows, :], corner], axis=0)


def forward_kernel(n, rows, me_ref, *refs):
    q_in, k_in, v_in = refs[:n], refs[n : 2 * n], refs[2 * n : 3 * n]
    rate_q, rate_k, gain_q, gain_k, cosine, sine = refs[3 * n : 3 * n + 6]
    attn, q_out, k_out, v_out, lse, turned_v = refs[3 * n + 6 :]
    me = me_ref[0]

    def place(s):
        return pl.multiple_of(lax.rem(me - s + n, n) * rows, rows)

    for s in range(n):
        at = pl.ds(place(s), rows)
        c, d = cosine[at, :], sine[at, :]
        for src, rate, gain, dst in (
            (q_in[s], rate_q, gain_q, q_out),
            (k_in[s], rate_k, gain_k, k_out),
        ):
            normed = src[...] * rate[at, :] * gain[0]
            turned = normed * c + pltpu.roll(normed, HD // 2, 1) * d
            dst[at, :] = turned.astype(BF)
        v_out[at, :] = v_in[s][...].astype(BF)
    turned_v[...] = v_out[...].T
    for piece in range(n):
        first, last = piece * rows, (piece + 1) * rows
        scores = masked_scores(k_out[:last, :], q_out[first:last, :], last, rows)
        peak = jnp.max(scores, axis=0, keepdims=True)
        grown = jnp.exp(scores - peak)
        total = jnp.sum(grown, axis=0, keepdims=True)
        lse[0, :, first:last] = peak + jnp.log(total)
        probs = (grown * (1.0 / total)).astype(BF)
        out = dot_plain(turned_v[:, :last], probs)
        attn[pl.ds(place(piece), rows), :] = out.T.astype(BF)


def backward_kernel(n, rows, me_ref, *refs):
    q_in, k_in, g_in = refs[:n], refs[n : 2 * n], refs[2 * n : 3 * n]
    (rate_q, rate_k, gain_q, gain_k, cosine, sine, q_rot, k_rot, value, lse) = refs[
        3 * n : 3 * n + 10
    ]
    t_q, t_k, d_v, sums, gains = refs[3 * n + 10 : 3 * n + 15]
    grads, turned_k, acc_q, acc_k, acc_v = refs[3 * n + 15 :]
    me = me_ref[0]
    scale = HD ** (-0.5)

    def place(s):
        return pl.multiple_of(lax.rem(me - s + n, n) * rows, rows)

    for s in range(n):
        grads[pl.ds(place(s), rows), :] = g_in[s][...]
    turned_k[...] = k_rot[...].T
    for piece in reversed(range(n)):
        first, last = piece * rows, (piece + 1) * rows
        queries, keys = q_rot[first:last, :], k_rot[:last, :]
        grad = grads[first:last, :]
        scores = masked_scores(keys, queries, last, rows)
        probs = jnp.exp(scores - lse[0, :, first:last])
        d_probs = dot_right_t(value[:last, :], grad)
        delta = jnp.sum(probs * d_probs, axis=0, keepdims=True)
        d_scores = (probs * (d_probs - delta) * scale).astype(BF)
        add_v = dot_plain(probs.astype(BF), grad)
        add_k = dot_plain(d_scores, queries)
        if piece == n - 1:
            acc_v[...] = add_v
            acc_k[...] = add_k
        else:
            acc_v[:last, :] += add_v
            acc_k[:last, :] += add_k
        acc_q[first:last, :] = dot_plain(turned_k[:, :last], d_scores).T
    ones = jnp.ones((8, HD), F32)
    head = pl.program_id(0)
    for which, (acc, src, rate, gain, out) in enumerate(
        ((acc_q, q_in, rate_q, gain_q, t_q), (acc_k, k_in, rate_k, gain_k, t_k))
    ):
        column = jnp.zeros((1, HD), F32)
        for s in range(n):
            at = pl.ds(place(s), rows)
            grad = acc[at, :]
            normed = grad * cosine[at, :] - pltpu.roll(grad, HD // 2, 1) * sine[at, :]
            hat = src[s][...] * rate[at, :]
            column = column + jnp.sum(normed * hat, axis=0, keepdims=True)
            scaled = normed * gain[0]
            out[s * rows : (s + 1) * rows, :] = scaled
            line = lax.dot_general(
                ones,
                scaled * hat,
                (((1,), (1,)), ((), ())),
                precision=lax.Precision.HIGHEST,
                preferred_element_type=F32,
            )
            here = (which, slice(None), slice(s * rows, (s + 1) * rows))

            @pl.when(head == 0)
            def _():
                sums[here] = line

            @pl.when(head > 0)
            def _():
                sums[here] += line

        gains[0, which : which + 1, :] = column
    for s in range(n):
        d_v[s * rows : (s + 1) * rows, :] = acc_v[pl.ds(place(s), rows), :].astype(BF)


def attention_forward(me, pieces, rate_q, rate_k, gain_q, gain_k, cosine, sine):
    n, rows = len(pieces), pieces[0].shape[0]
    heads = gain_q.shape[0]

    def part(offset):
        return [pl.BlockSpec((rows, HD), lambda h, m, o=offset: (0, o * heads + h))] * n

    whole = pl.BlockSpec((L, HD), lambda h, m: (0, 0))
    gain = pl.BlockSpec((1, 1, HD), lambda h, m: (h, 0, 0))
    column = pl.BlockSpec((L, HD), lambda h, m: (0, h))
    low = jax.ShapeDtypeStruct((L, heads * HD), BF)
    return pl.pallas_call(
        functools.partial(forward_kernel, n, rows),
        grid_spec=pltpu.PrefetchScalarGridSpec(
            num_scalar_prefetch=1,
            grid=(heads,),
            in_specs=part(0) + part(1) + part(2) + [whole, whole, gain, gain, whole, whole],
            out_specs=[column] * 4 + [pl.BlockSpec((1, 1, L), lambda h, m: (h, 0, 0))],
            scratch_shapes=[pltpu.VMEM((HD, L), BF)],
        ),
        out_shape=[low] * 4 + [jax.ShapeDtypeStruct((heads, 1, L), F32)],
        compiler_params=pltpu.CompilerParams(vmem_limit_bytes=48 << 20),
        cost_estimate=pl.CostEstimate(
            flops=2 * heads * L * L * HD,
            bytes_accessed=12 * heads * L * HD + 10 * heads * L * HD,
            transcendentals=heads * L * L // 2,
        ),
        name="attention_forward",
    )(
        me,
        *pieces,
        *pieces,
        *pieces,
        rate_q,
        rate_k,
        gain_q[:, None, :],
        gain_k[:, None, :],
        cosine,
        sine,
    )


def attention_backward(
    me, pieces, grads, rate_q, rate_k, gain_q, gain_k, cosine, sine, q_rot, k_rot, value, lse
):
    n, rows = len(pieces), pieces[0].shape[0]
    heads = gain_q.shape[0]

    def part(offset):
        return [pl.BlockSpec((rows, HD), lambda h, m, o=offset: (0, o * heads + h))] * n

    whole = pl.BlockSpec((L, HD), lambda h, m: (0, 0))
    gain = pl.BlockSpec((1, 1, HD), lambda h, m: (h, 0, 0))
    column = pl.BlockSpec((L, HD), lambda h, m: (0, h))
    wide = jax.ShapeDtypeStruct((L, heads * HD), F32)
    return pl.pallas_call(
        functools.partial(backward_kernel, n, rows),
        grid_spec=pltpu.PrefetchScalarGridSpec(
            num_scalar_prefetch=1,
            grid=(heads,),
            in_specs=part(0)
            + part(1)
            + part(0)
            + [whole, whole, gain, gain, whole, whole]
            + [column] * 3
            + [pl.BlockSpec((1, 1, L), lambda h, m: (h, 0, 0))],
            out_specs=[column] * 3
            + [
                pl.BlockSpec((2, 8, L), lambda h, m: (0, 0, 0)),
                pl.BlockSpec((1, 2, HD), lambda h, m: (h, 0, 0)),
            ],
            scratch_shapes=[
                pltpu.VMEM((L, HD), BF),
                pltpu.VMEM((HD, L), BF),
                pltpu.VMEM((L, HD), F32),
                pltpu.VMEM((L, HD), F32),
                pltpu.VMEM((L, HD), F32),
            ],
        ),
        out_shape=[
            wide,
            wide,
            jax.ShapeDtypeStruct((L, heads * HD), BF),
            jax.ShapeDtypeStruct((2, 8, L), F32),
            jax.ShapeDtypeStruct((heads, 2, HD), F32),
        ],
        compiler_params=pltpu.CompilerParams(vmem_limit_bytes=48 << 20),
        cost_estimate=pl.CostEstimate(
            flops=5 * heads * L * L * HD,
            bytes_accessed=26 * heads * L * HD,
            transcendentals=heads * L * L // 2,
        ),
        name="attention_backward",
    )(
        me,
        *pieces,
        *pieces,
        *grads,
        rate_q,
        rate_k,
        gain_q[:, None, :],
        gain_k[:, None, :],
        cosine,
        sine,
        q_rot,
        k_rot,
        value,
        lse,
    )


def weight_kernel(n, *refs):
    x_in, d_in, a_in = refs[:n], refs[n : 2 * n], refs[2 * n : 3 * n]
    attn, out = refs[3 * n :]
    rows, wide = d_in[0].shape
    one = sum(dot_left_t(x_in[s][...], d_in[s][...]) for s in range(n))
    out[:, :wide] = one.astype(BF)
    two = sum(
        dot_left_t(a_in[s][...], attn[s * rows : (s + 1) * rows, :]) for s in range(n)
    )
    out[:, wide:] = two.astype(BF)


def attention_weights(held_x, d_qkv, held_a, attn):
    n, (rows, wide) = len(held_x), d_qkv[0].shape
    width, narrow = held_x[0].shape[1], attn.shape[1]
    tile = min(256, width)
    step = pl.BlockSpec((rows, tile), lambda i: (0, i))
    once = [pl.BlockSpec((rows, wide), lambda i: (0, 0), pipeline_mode=pl.Buffered(1))]
    return pl.pallas_call(
        functools.partial(weight_kernel, n),
        grid=(width // tile,),
        in_specs=[step] * n
        + once * n
        + [step] * n
        + [pl.BlockSpec((n * rows, narrow), lambda i: (0, 0), pipeline_mode=pl.Buffered(1))],
        out_specs=pl.BlockSpec((tile, wide + narrow), lambda i: (i, 0)),
        out_shape=jax.ShapeDtypeStruct((width, wide + narrow), BF),
        compiler_params=pltpu.CompilerParams(vmem_limit_bytes=40 << 20),
        cost_estimate=pl.CostEstimate(
            flops=2 * n * rows * width * (wide + narrow),
            bytes_accessed=2 * (width + n * rows) * (wide + narrow) + 4 * n * rows * width,
            transcendentals=0,
        ),
        name="attention_weights",
    )(*held_x, *d_qkv, *held_a, attn)


def local(
    n,
    groups,
    inputs,
    w_query,
    w_key,
    w_value,
    q_gain,
    k_gain,
    w_out,
    attn_gain,
    w_gate,
    w_up,
    w_down,
    mlp_gain,
    cotangent,
):
    rows, width = inputs.shape
    heads, slice_q = q_gain.shape
    head_cols = heads * HD
    units = w_gate.shape[1]
    me = lax.axis_index("mp").astype(jnp.int32)
    me_ref = me.reshape(1)
    ring = [(i, (i + 1) % n) for i in range(n)]

    def shift(value):
        return lax.ppermute(value, "mp", ring)

    def sum_all(value):
        total = value
        for k in range(1, n):
            total = total + lax.ppermute(value, "mp", [(i, (i + k) % n) for i in range(n)])
        return total

    def reorder(stacked):
        turned = stacked[::-1]
        return lax.dynamic_slice_in_dim(
            jnp.concatenate([turned, turned], axis=0), n - 1 - me, n, axis=0
        )

    def gather_ring(own, first=1, last=n - 1, after={}):
        held = [own]
        for s in range(first, last + 1):
            sent = held[-1]
            if s in after:
                sent = lax.optimization_barrier((sent, after[s]))[0]
            held.append(shift(sent))
        return held

    def scatter_ring(partial_of, after={}):
        running = None
        for s in range(1, n):
            term = partial_of(s)
            if running is not None:
                term = term + running.astype(F32)
            term = term.astype(BF)
            if s in after:
                term = lax.optimization_barrier((term, after[s]))[0]
            running = shift(term)
        return partial_of(0) + running.astype(F32)

    w_attn = lax.all_gather(
        row_major(jnp.concatenate([w_query, w_key, w_value, row_major(w_out.T)], axis=1)),
        "dp",
        axis=0,
        tiled=True,
    )
    w_qkv = w_attn[:, : 3 * head_cols]
    out_t = w_attn[:, 3 * head_cols :]
    small = jnp.concatenate(
        [q_gain.reshape(-1), k_gain.reshape(-1), attn_gain, mlp_gain], axis=0
    )
    small = lax.all_gather(small, "dp", axis=0, tiled=False).astype(F32)
    count = heads * slice_q
    gain_q = small[:, :count].reshape(groups, heads, slice_q).transpose(1, 0, 2).reshape(heads, HD)
    gain_k = (
        small[:, count : 2 * count]
        .reshape(groups, heads, slice_q)
        .transpose(1, 0, 2)
        .reshape(heads, HD)
    )
    own_cols = attn_gain.shape[0]
    gain_a = small[:, 2 * count : 2 * count + own_cols].reshape(width)
    gain_m = small[:, 2 * count + own_cols :].reshape(width)
    full_gate = lax.all_gather(w_gate, "dp", axis=0, tiled=True)
    full_up = lax.all_gather(w_up, "dp", axis=0, tiled=True)
    full_down = lax.all_gather(w_down, "dp", axis=1, tiled=True)
    cosine, sine = rope_tables()

    held_x = gather_ring(inputs)
    pieces = []
    for x in held_x:
        pieces.append(dot_plain(x, w_qkv))
    squares = jnp.stack(
        [
            jnp.stack(
                [
                    jnp.sum(jnp.square(p[:, :head_cols]), axis=1),
                    jnp.sum(jnp.square(p[:, head_cols : 2 * head_cols]), axis=1),
                ]
            )
            for p in pieces
        ]
    )
    squares = sum_all(reorder(squares))
    rates = lax.rsqrt(squares / width + epsilon)
    rate_q = jnp.broadcast_to(rates[:, 0].reshape(L, 1), (L, HD))
    rate_k = jnp.broadcast_to(rates[:, 1].reshape(L, 1), (L, HD))
    attn, q_rot, k_rot, value, lse = attention_forward(
        me_ref, pieces, rate_q, rate_k, gain_q, gain_k, cosine, sine
    )
    attn_proj = scatter_ring(lambda s: dot_right_t(attn[s * rows : (s + 1) * rows], out_t))
    rate_a = lax.rsqrt(jnp.mean(attn_proj * attn_proj, axis=1, keepdims=True) + epsilon)
    hat_a = attn_proj * rate_a
    resid = inputs.astype(F32) + hat_a * gain_a
    resid_low = resid.astype(BF)

    held_r = gather_ring(resid_low)
    gates, ups, hiddens = [], [], []
    for r in held_r:
        gate = dot_plain(r, full_gate)
        up = dot_plain(r, full_up)
        gates.append(gate)
        ups.append(up)
        hiddens.append((gate * jax.nn.sigmoid(gate) * up).astype(BF))
    mlp_proj = scatter_ring(lambda s: dot_plain(hiddens[s], full_down))
    rate_m = lax.rsqrt(jnp.mean(mlp_proj * mlp_proj, axis=1, keepdims=True) + epsilon)
    hat_m = mlp_proj * rate_m
    output = resid + hat_m * gain_m

    upstream = cotangent.astype(F32)
    grad_gain_m = jnp.sum(upstream * hat_m, axis=0)
    scaled_m = upstream * gain_m
    d_mlp = (
        rate_m * (scaled_m - hat_m * jnp.mean(scaled_m * hat_m, axis=1, keepdims=True))
    ).astype(BF)
    held_m = gather_ring(d_mlp)
    d_gates, d_ups = [], []
    for s in range(n):
        gate, up = gates[s], ups[s]
        sigma = jax.nn.sigmoid(gate)
        d_hidden = dot_right_t(held_m[s], full_down)
        d_gates.append((d_hidden * up * sigma * (1.0 + gate * (1.0 - sigma))).astype(BF))
        d_ups.append((d_hidden * (gate * sigma)).astype(BF))
    down = dot_left_t(jnp.concatenate(hiddens, axis=0), jnp.concatenate(held_m, axis=0)).astype(BF)
    d_resid = upstream + scatter_ring(
        lambda s: dot_right_t(d_gates[s], full_gate) + dot_right_t(d_ups[s], full_up),
        {1: held_m[-1]},
    )
    grad_down = lax.psum_scatter(down, "dp", scatter_dimension=1, tiled=True)
    d_gate_up = jnp.concatenate(
        [jnp.concatenate(d_gates, axis=0), jnp.concatenate(d_ups, axis=0)], axis=1
    )
    all_r = jnp.concatenate(held_r, axis=0)
    gate_up = dot_left_t(all_r, d_gate_up).astype(BF)

    grad_gain_a = jnp.sum(d_resid * hat_a, axis=0)
    scaled_a = d_resid * gain_a
    d_attn_proj = (
        rate_a * (scaled_a - hat_a * jnp.mean(scaled_a * hat_a, axis=1, keepdims=True))
    ).astype(BF)
    held_a = gather_ring(d_attn_proj, after={max(n - 2, 1): grad_down})
    grad_gate_up = lax.psum_scatter(gate_up, "dp", scatter_dimension=0, tiled=True)
    d_attn = [dot_plain(a, out_t).astype(BF) for a in held_a]
    t_q, t_k, d_value, sums, head_gains = attention_backward(
        me_ref,
        pieces,
        d_attn,
        rate_q,
        rate_k,
        gain_q,
        gain_k,
        cosine,
        sine,
        q_rot,
        k_rot,
        value,
        lse,
    )
    sums = reorder(sums[:, 0, :].reshape(2, n, rows).transpose(1, 0, 2))
    sums = sum_all(sums)
    back = reorder(jnp.concatenate([rates, sums / width], axis=1))
    d_qkv = []
    for s in range(n):
        at = slice(s * rows, (s + 1) * rows)
        parts = []
        for which, t in enumerate((t_q, t_k)):
            rate = back[s, which][:, None]
            raw = pieces[s][:, which * head_cols : (which + 1) * head_cols]
            parts.append((rate * (t[at] - raw * (rate * back[s, 2 + which][:, None]))).astype(BF))
        parts.append(d_value[at])
        d_qkv.append(jnp.concatenate(parts, axis=1))
    dw_attn = attention_weights(held_x, d_qkv, held_a, attn)
    grad_attn = lax.psum_scatter(dw_attn, "dp", scatter_dimension=0, tiled=True)
    input_grad = d_resid + scatter_ring(
        lambda s: dot_right_t(d_qkv[s], w_qkv), {n - 1: grad_gate_up}
    )

    grad_attn, input_grad = lax.optimization_barrier((grad_attn, input_grad))
    grad_query = grad_attn[:, :head_cols].astype(F32)
    grad_key = grad_attn[:, head_cols : 2 * head_cols].astype(F32)
    grad_value = grad_attn[:, 2 * head_cols : 3 * head_cols].astype(F32)
    grad_out = grad_attn[:, 3 * head_cols :].astype(F32).T
    grad_gate = grad_gate_up[:, :units].astype(F32)
    grad_up = grad_gate_up[:, units:].astype(F32)

    post = lax.psum(jnp.stack([grad_gain_a, grad_gain_m]), "mp")
    post = post.reshape(2, groups, own_cols).transpose(1, 0, 2).reshape(groups, 2 * own_cols)
    own = head_gains.transpose(1, 0, 2).reshape(2, heads, groups, slice_q)
    own = own.transpose(2, 0, 1, 3).reshape(groups, 2 * count)
    totals = lax.psum(jnp.concatenate([own, post], axis=1), "dp")
    mine = lax.dynamic_index_in_dim(totals, lax.axis_index("dp"), 0, keepdims=False)
    return (
        output,
        input_grad,
        grad_query,
        grad_key,
        grad_value,
        mine[:count].reshape(heads, slice_q),
        mine[count : 2 * count].reshape(heads, slice_q),
        grad_out,
        mine[2 * count : 2 * count + own_cols],
        grad_gate,
        grad_up,
        grad_down.astype(F32),
        mine[2 * count + own_cols :],
    )


def solution(mesh):
    in_specs = (
        P(("dp", "mp"), None),
        P("dp", "mp"),
        P("dp", "mp"),
        P("dp", "mp"),
        P("mp", "dp"),
        P("mp", "dp"),
        P("mp", "dp"),
        P("dp"),
        P("dp", "mp"),
        P("dp", "mp"),
        P("mp", "dp"),
        P("dp"),
        P(("dp", "mp"), None),
    )
    out_specs = (
        P(("dp", "mp"), None),
        P(("dp", "mp"), None),
        P("dp", "mp"),
        P("dp", "mp"),
        P("dp", "mp"),
        P("mp", "dp"),
        P("mp", "dp"),
        P("mp", "dp"),
        P("dp"),
        P("dp", "mp"),
        P("dp", "mp"),
        P("mp", "dp"),
        P("dp"),
    )

    def body(*args):
        return local(mesh.shape["mp"], mesh.shape["dp"], *args)

    return jax.shard_map(body, mesh=mesh, in_specs=in_specs, out_specs=out_specs, check_vma=False)
```

```python
import functools

import jax
import jax.numpy as jnp
from jax import lax
from jax.experimental import pallas as pl
from jax.experimental.layout import Layout, with_layout_constraint
from jax.experimental.pallas import tpu as pltpu
from jax.sharding import PartitionSpec as P


HD = 128
L = 1024

epsilon = 1e-06
rope_base = 500000.0

BF = jnp.bfloat16
F32 = jnp.float32


def dot_plain(left, right):
    return jnp.dot(left, right, preferred_element_type=F32)


def dot_right_t(left, right):
    return lax.dot_general(left, right, (((1,), (1,)), ((), ())), preferred_element_type=F32)


def dot_left_t(left, right):
    return lax.dot_general(left, right, (((0,), (0,)), ((), ())), preferred_element_type=F32)


def row_major(value):
    return with_layout_constraint(value, Layout(major_to_minor=(0, 1)))


def rope_tables():
    half = HD // 2
    freqs = rope_base ** (-2.0 * jnp.arange(half, dtype=F32) / HD)
    angles = jnp.arange(L).astype(F32)[:, None] * freqs[None, :]
    cosine, sine = jnp.cos(angles), jnp.sin(angles)
    return (
        jnp.concatenate([cosine, cosine], axis=1),
        jnp.concatenate([-sine, sine], axis=1),
    )


def masked_scores(keys, queries, last, rows):
    scores = dot_right_t(keys, queries) * (HD ** (-0.5))
    row = lax.broadcasted_iota(jnp.int32, (rows, rows), 0)
    col = lax.broadcasted_iota(jnp.int32, (rows, rows), 1)
    corner = jnp.where(row <= col, scores[last - rows :, :], -1e30)
    if last == rows:
        return corner
    return jnp.concatenate([scores[: last - rows, :], corner], axis=0)


def forward_kernel(n, rows, me_ref, *refs):
    q_in, k_in, v_in = refs[:n], refs[n : 2 * n], refs[2 * n : 3 * n]
    rate_q, rate_k, gain_q, gain_k, cosine, sine = refs[3 * n : 3 * n + 6]
    attn, q_out, k_out, v_out, lse, turned_v = refs[3 * n + 6 :]
    me = me_ref[0]

    def place(s):
        return pl.multiple_of(lax.rem(me - s + n, n) * rows, rows)

    for s in range(n):
        at = pl.ds(place(s), rows)
        c, d = cosine[at, :], sine[at, :]
        for src, rate, gain, dst in (
            (q_in[s], rate_q, gain_q, q_out),
            (k_in[s], rate_k, gain_k, k_out),
        ):
            normed = src[...] * rate[at, :] * gain[0]
            turned = normed * c + pltpu.roll(normed, HD // 2, 1) * d
            dst[at, :] = turned.astype(BF)
        v_out[at, :] = v_in[s][...].astype(BF)
    turned_v[...] = v_out[...].T
    for piece in range(n):
        first, last = piece * rows, (piece + 1) * rows
        scores = masked_scores(k_out[:last, :], q_out[first:last, :], last, rows)
        peak = jnp.max(scores, axis=0, keepdims=True)
        grown = jnp.exp(scores - peak)
        total = jnp.sum(grown, axis=0, keepdims=True)
        lse[0, :, first:last] = peak + jnp.log(total)
        probs = (grown * (1.0 / total)).astype(BF)
        out = dot_plain(turned_v[:, :last], probs)
        attn[pl.ds(place(piece), rows), :] = out.T.astype(BF)


def backward_kernel(n, rows, me_ref, *refs):
    q_in, k_in, g_in = refs[:n], refs[n : 2 * n], refs[2 * n : 3 * n]
    (rate_q, rate_k, gain_q, gain_k, cosine, sine, q_rot, k_rot, value, lse) = refs[
        3 * n : 3 * n + 10
    ]
    t_q, t_k, d_v, sums, gains = refs[3 * n + 10 : 3 * n + 15]
    grads, turned_k, acc_q, acc_k, acc_v, acc_sums = refs[3 * n + 15 :]
    me = me_ref[0]
    scale = HD ** (-0.5)

    def place(s):
        return pl.multiple_of(lax.rem(me - s + n, n) * rows, rows)

    for s in range(n):
        grads[pl.ds(place(s), rows), :] = g_in[s][...]
    turned_k[...] = k_rot[...].T
    for piece in reversed(range(n)):
        first, last = piece * rows, (piece + 1) * rows
        queries, keys = q_rot[first:last, :], k_rot[:last, :]
        grad = grads[first:last, :]
        scores = masked_scores(keys, queries, last, rows)
        probs = jnp.exp(scores - lse[0, :, first:last])
        d_probs = dot_right_t(value[:last, :], grad)
        delta = jnp.sum(probs * d_probs, axis=0, keepdims=True)
        d_scores = (probs * (d_probs - delta) * scale).astype(BF)
        add_v = dot_plain(probs.astype(BF), grad)
        add_k = dot_plain(d_scores, queries)
        if piece == n - 1:
            acc_v[...] = add_v
            acc_k[...] = add_k
        else:
            acc_v[:last, :] += add_v
            acc_k[:last, :] += add_k
        acc_q[first:last, :] = dot_plain(turned_k[:, :last], d_scores).T
    head = pl.program_id(0)

    @pl.when(head == 0)
    def _():
        acc_sums[...] = jnp.zeros_like(acc_sums)

    for which, (acc, src, rate, gain, out) in enumerate(
        ((acc_q, q_in, rate_q, gain_q, t_q), (acc_k, k_in, rate_k, gain_k, t_k))
    ):
        column = jnp.zeros((1, HD), F32)
        for s in range(n):
            at = pl.ds(place(s), rows)
            grad = acc[at, :]
            normed = grad * cosine[at, :] - pltpu.roll(grad, HD // 2, 1) * sine[at, :]
            hat = src[s][...] * rate[at, :]
            column = column + jnp.sum(normed * hat, axis=0, keepdims=True)
            scaled = normed * gain[0]
            here = slice(s * rows, (s + 1) * rows)
            out[here, :] = scaled
            acc_sums[which, here, :] += scaled * hat
        gains[0, which : which + 1, :] = column
    for s in range(n):
        d_v[s * rows : (s + 1) * rows, :] = acc_v[pl.ds(place(s), rows), :].astype(BF)

    @pl.when(head == pl.num_programs(0) - 1)
    def _():
        for which in range(2):
            sums[which] = jnp.sum(acc_sums[which].T, axis=0, keepdims=True)


def attention_forward(me, pieces, rate_q, rate_k, gain_q, gain_k, cosine, sine):
    n, rows = len(pieces), pieces[0].shape[0]
    heads = gain_q.shape[0]

    def part(offset):
        return [pl.BlockSpec((rows, HD), lambda h, m, o=offset: (0, o * heads + h))] * n

    whole = pl.BlockSpec((L, HD), lambda h, m: (0, 0))
    gain = pl.BlockSpec((1, 1, HD), lambda h, m: (h, 0, 0))
    column = pl.BlockSpec((L, HD), lambda h, m: (0, h))
    low = jax.ShapeDtypeStruct((L, heads * HD), BF)
    return pl.pallas_call(
        functools.partial(forward_kernel, n, rows),
        grid_spec=pltpu.PrefetchScalarGridSpec(
            num_scalar_prefetch=1,
            grid=(heads,),
            in_specs=part(0) + part(1) + part(2) + [whole, whole, gain, gain, whole, whole],
            out_specs=[column] * 4 + [pl.BlockSpec((1, 1, L), lambda h, m: (h, 0, 0))],
            scratch_shapes=[pltpu.VMEM((HD, L), BF)],
        ),
        out_shape=[low] * 4 + [jax.ShapeDtypeStruct((heads, 1, L), F32)],
        compiler_params=pltpu.CompilerParams(vmem_limit_bytes=48 << 20),
        cost_estimate=pl.CostEstimate(
            flops=2 * heads * L * L * HD,
            bytes_accessed=12 * heads * L * HD + 10 * heads * L * HD,
            transcendentals=heads * L * L // 2,
        ),
        name="attention_forward",
    )(
        me,
        *pieces,
        *pieces,
        *pieces,
        rate_q,
        rate_k,
        gain_q[:, None, :],
        gain_k[:, None, :],
        cosine,
        sine,
    )


def attention_backward(
    me, pieces, grads, rate_q, rate_k, gain_q, gain_k, cosine, sine, q_rot, k_rot, value, lse
):
    n, rows = len(pieces), pieces[0].shape[0]
    heads = gain_q.shape[0]

    def part(offset):
        return [pl.BlockSpec((rows, HD), lambda h, m, o=offset: (0, o * heads + h))] * n

    whole = pl.BlockSpec((L, HD), lambda h, m: (0, 0))
    gain = pl.BlockSpec((1, 1, HD), lambda h, m: (h, 0, 0))
    column = pl.BlockSpec((L, HD), lambda h, m: (0, h))
    wide = jax.ShapeDtypeStruct((L, heads * HD), F32)
    return pl.pallas_call(
        functools.partial(backward_kernel, n, rows),
        grid_spec=pltpu.PrefetchScalarGridSpec(
            num_scalar_prefetch=1,
            grid=(heads,),
            in_specs=part(0)
            + part(1)
            + part(0)
            + [whole, whole, gain, gain, whole, whole]
            + [column] * 3
            + [pl.BlockSpec((1, 1, L), lambda h, m: (h, 0, 0))],
            out_specs=[column] * 3
            + [
                pl.BlockSpec((2, 1, L), lambda h, m: (0, 0, 0)),
                pl.BlockSpec((1, 2, HD), lambda h, m: (h, 0, 0)),
            ],
            scratch_shapes=[
                pltpu.VMEM((L, HD), BF),
                pltpu.VMEM((HD, L), BF),
                pltpu.VMEM((L, HD), F32),
                pltpu.VMEM((L, HD), F32),
                pltpu.VMEM((L, HD), F32),
                pltpu.VMEM((2, L, HD), F32),
            ],
        ),
        out_shape=[
            wide,
            wide,
            jax.ShapeDtypeStruct((L, heads * HD), BF),
            jax.ShapeDtypeStruct((2, 1, L), F32),
            jax.ShapeDtypeStruct((heads, 2, HD), F32),
        ],
        compiler_params=pltpu.CompilerParams(vmem_limit_bytes=48 << 20),
        cost_estimate=pl.CostEstimate(
            flops=5 * heads * L * L * HD,
            bytes_accessed=26 * heads * L * HD,
            transcendentals=heads * L * L // 2,
        ),
        name="attention_backward",
    )(
        me,
        *pieces,
        *pieces,
        *grads,
        rate_q,
        rate_k,
        gain_q[:, None, :],
        gain_k[:, None, :],
        cosine,
        sine,
        q_rot,
        k_rot,
        value,
        lse,
    )


def weight_kernel(n, *refs):
    x_in, d_in, a_in = refs[:n], refs[n : 2 * n], refs[2 * n : 3 * n]
    attn, out = refs[3 * n :]
    rows, wide = d_in[0].shape
    one = sum(dot_left_t(x_in[s][...], d_in[s][...]) for s in range(n))
    out[:, :wide] = one.astype(BF)
    two = sum(
        dot_left_t(a_in[s][...], attn[s * rows : (s + 1) * rows, :]) for s in range(n)
    )
    out[:, wide:] = two.astype(BF)


def attention_weights(held_x, d_qkv, held_a, attn):
    n, (rows, wide) = len(held_x), d_qkv[0].shape
    width, narrow = held_x[0].shape[1], attn.shape[1]
    tile = min(256, width)
    step = pl.BlockSpec((rows, tile), lambda i: (0, i))
    once = [pl.BlockSpec((rows, wide), lambda i: (0, 0), pipeline_mode=pl.Buffered(1))]
    return pl.pallas_call(
        functools.partial(weight_kernel, n),
        grid=(width // tile,),
        in_specs=[step] * n
        + once * n
        + [step] * n
        + [pl.BlockSpec((n * rows, narrow), lambda i: (0, 0), pipeline_mode=pl.Buffered(1))],
        out_specs=pl.BlockSpec((tile, wide + narrow), lambda i: (i, 0)),
        out_shape=jax.ShapeDtypeStruct((width, wide + narrow), BF),
        compiler_params=pltpu.CompilerParams(vmem_limit_bytes=40 << 20),
        cost_estimate=pl.CostEstimate(
            flops=2 * n * rows * width * (wide + narrow),
            bytes_accessed=2 * (width + n * rows) * (wide + narrow) + 4 * n * rows * width,
            transcendentals=0,
        ),
        name="attention_weights",
    )(*held_x, *d_qkv, *held_a, attn)


def local(
    n,
    groups,
    inputs,
    w_query,
    w_key,
    w_value,
    q_gain,
    k_gain,
    w_out,
    attn_gain,
    w_gate,
    w_up,
    w_down,
    mlp_gain,
    cotangent,
):
    rows, width = inputs.shape
    heads, slice_q = q_gain.shape
    head_cols = heads * HD
    units = w_gate.shape[1]
    me = lax.axis_index("mp").astype(jnp.int32)
    me_ref = me.reshape(1)
    ring = [(i, (i + 1) % n) for i in range(n)]

    def shift(value):
        return lax.ppermute(value, "mp", ring)

    def sum_all(value):
        total = value
        for k in range(1, n):
            total = total + lax.ppermute(value, "mp", [(i, (i + k) % n) for i in range(n)])
        return total

    def reorder(stacked):
        turned = stacked[::-1]
        return lax.dynamic_slice_in_dim(
            jnp.concatenate([turned, turned], axis=0), n - 1 - me, n, axis=0
        )

    def gather_ring(own, first=1, last=n - 1, after={}):
        held = [own]
        for s in range(first, last + 1):
            sent = held[-1]
            if s in after:
                sent = lax.optimization_barrier((sent, after[s]))[0]
            held.append(shift(sent))
        return held

    def scatter_ring(partial_of, after={}):
        running = None
        for s in range(1, n):
            term = partial_of(s)
            if running is not None:
                term = term + running.astype(F32)
            term = term.astype(BF)
            if s in after:
                term = lax.optimization_barrier((term, after[s]))[0]
            running = shift(term)
        return partial_of(0) + running.astype(F32)

    w_attn = lax.all_gather(
        row_major(jnp.concatenate([w_query, w_key, w_value, row_major(w_out.T)], axis=1)),
        "dp",
        axis=0,
        tiled=True,
    )
    w_qkv = w_attn[:, : 3 * head_cols]
    out_t = w_attn[:, 3 * head_cols :]
    small = jnp.concatenate(
        [q_gain.reshape(-1), k_gain.reshape(-1), attn_gain, mlp_gain], axis=0
    )
    small = lax.all_gather(small, "dp", axis=0, tiled=False).astype(F32)
    count = heads * slice_q
    gain_q = small[:, :count].reshape(groups, heads, slice_q).transpose(1, 0, 2).reshape(heads, HD)
    gain_k = (
        small[:, count : 2 * count]
        .reshape(groups, heads, slice_q)
        .transpose(1, 0, 2)
        .reshape(heads, HD)
    )
    own_cols = attn_gain.shape[0]
    gain_a = small[:, 2 * count : 2 * count + own_cols].reshape(width)
    gain_m = small[:, 2 * count + own_cols :].reshape(width)
    full_gate_up = lax.all_gather(
        jnp.concatenate([w_gate, w_up], axis=1), "dp", axis=0, tiled=True
    )
    full_gate, full_up = full_gate_up[:, :units], full_gate_up[:, units:]
    full_down = lax.all_gather(w_down, "dp", axis=1, tiled=True)
    cosine, sine = rope_tables()

    held_x = gather_ring(inputs)
    pieces = []
    for x in held_x:
        pieces.append(dot_plain(x, w_qkv))
    squares = jnp.stack(
        [
            jnp.stack(
                [
                    jnp.sum(jnp.square(p[:, :head_cols]), axis=1),
                    jnp.sum(jnp.square(p[:, head_cols : 2 * head_cols]), axis=1),
                ]
            )
            for p in pieces
        ]
    )
    squares = sum_all(reorder(squares))
    rates = lax.rsqrt(squares / width + epsilon)
    rate_q = jnp.broadcast_to(rates[:, 0].reshape(L, 1), (L, HD))
    rate_k = jnp.broadcast_to(rates[:, 1].reshape(L, 1), (L, HD))
    attn, q_rot, k_rot, value, lse = attention_forward(
        me_ref, pieces, rate_q, rate_k, gain_q, gain_k, cosine, sine
    )
    attn_proj = scatter_ring(lambda s: dot_right_t(attn[s * rows : (s + 1) * rows], out_t))
    rate_a = lax.rsqrt(jnp.mean(attn_proj * attn_proj, axis=1, keepdims=True) + epsilon)
    hat_a = attn_proj * rate_a
    resid = inputs.astype(F32) + hat_a * gain_a
    resid_low = resid.astype(BF)

    held_r = gather_ring(resid_low)
    gates, ups, hiddens = [], [], []
    for r in held_r:
        gate = dot_plain(r, full_gate)
        up = dot_plain(r, full_up)
        gates.append(gate)
        ups.append(up)
        hiddens.append((gate * jax.nn.sigmoid(gate) * up).astype(BF))
    mlp_proj = scatter_ring(lambda s: dot_plain(hiddens[s], full_down))
    rate_m = lax.rsqrt(jnp.mean(mlp_proj * mlp_proj, axis=1, keepdims=True) + epsilon)
    hat_m = mlp_proj * rate_m
    output = resid + hat_m * gain_m

    upstream = cotangent.astype(F32)
    grad_gain_m = jnp.sum(upstream * hat_m, axis=0)
    scaled_m = upstream * gain_m
    d_mlp = (
        rate_m * (scaled_m - hat_m * jnp.mean(scaled_m * hat_m, axis=1, keepdims=True))
    ).astype(BF)
    held_m = gather_ring(d_mlp)
    d_gates, d_ups = [], []
    for s in range(n):
        gate, up = gates[s], ups[s]
        sigma = jax.nn.sigmoid(gate)
        d_hidden = dot_right_t(held_m[s], full_down)
        d_gates.append((d_hidden * up * sigma * (1.0 + gate * (1.0 - sigma))).astype(BF))
        d_ups.append((d_hidden * (gate * sigma)).astype(BF))
    down = dot_left_t(jnp.concatenate(hiddens, axis=0), jnp.concatenate(held_m, axis=0)).astype(BF)
    d_resid = upstream + scatter_ring(
        lambda s: dot_right_t(d_gates[s], full_gate) + dot_right_t(d_ups[s], full_up),
        {1: held_m[-1]},
    )
    grad_down = lax.psum_scatter(down, "dp", scatter_dimension=1, tiled=True)
    d_gate_up = jnp.concatenate(
        [jnp.concatenate(d_gates, axis=0), jnp.concatenate(d_ups, axis=0)], axis=1
    )
    all_r = jnp.concatenate(held_r, axis=0)
    gate_up = dot_left_t(all_r, d_gate_up).astype(BF)

    grad_gain_a = jnp.sum(d_resid * hat_a, axis=0)
    scaled_a = d_resid * gain_a
    d_attn_proj = (
        rate_a * (scaled_a - hat_a * jnp.mean(scaled_a * hat_a, axis=1, keepdims=True))
    ).astype(BF)
    held_a = gather_ring(d_attn_proj, after={n - 1: grad_down})
    grad_gate_up = lax.psum_scatter(gate_up, "dp", scatter_dimension=0, tiled=True)
    d_attn = [dot_plain(a, out_t).astype(BF) for a in held_a]
    t_q, t_k, d_value, sums, head_gains = attention_backward(
        me_ref,
        pieces,
        d_attn,
        rate_q,
        rate_k,
        gain_q,
        gain_k,
        cosine,
        sine,
        q_rot,
        k_rot,
        value,
        lse,
    )
    sums = reorder(sums[:, 0, :].reshape(2, n, rows).transpose(1, 0, 2))
    sums = sum_all(sums)
    back = reorder(jnp.concatenate([rates, sums / width], axis=1))
    d_qkv = []
    for s in range(n):
        at = slice(s * rows, (s + 1) * rows)
        parts = []
        for which, t in enumerate((t_q, t_k)):
            rate = back[s, which][:, None]
            raw = pieces[s][:, which * head_cols : (which + 1) * head_cols]
            parts.append((rate * (t[at] - raw * (rate * back[s, 2 + which][:, None]))).astype(BF))
        parts.append(d_value[at])
        d_qkv.append(jnp.concatenate(parts, axis=1))
    dw_attn = attention_weights(held_x, d_qkv, held_a, attn)
    grad_attn = lax.psum_scatter(dw_attn, "dp", scatter_dimension=0, tiled=True)
    input_grad = d_resid + scatter_ring(
        lambda s: dot_right_t(d_qkv[s], w_qkv), {n - 1: grad_gate_up}
    )

    grad_attn, input_grad = lax.optimization_barrier((grad_attn, input_grad))
    grad_query = grad_attn[:, :head_cols].astype(F32)
    grad_key = grad_attn[:, head_cols : 2 * head_cols].astype(F32)
    grad_value = grad_attn[:, 2 * head_cols : 3 * head_cols].astype(F32)
    grad_out = grad_attn[:, 3 * head_cols :].astype(F32).T
    grad_gate = grad_gate_up[:, :units].astype(F32)
    grad_up = grad_gate_up[:, units:].astype(F32)

    post = sum_all(jnp.stack([grad_gain_a, grad_gain_m]))
    post = post.reshape(2, groups, own_cols).transpose(1, 0, 2).reshape(groups, 2 * own_cols)
    own = head_gains.transpose(1, 0, 2).reshape(2, heads, groups, slice_q)
    own = own.transpose(2, 0, 1, 3).reshape(groups, 2 * count)
    totals = jnp.concatenate([own, post], axis=1)
    if groups & (groups - 1):
        totals = lax.psum(totals, "dp")
    else:
        for k in range(groups.bit_length() - 1):
            pairs = [(i, i ^ (1 << k)) for i in range(groups)]
            totals = totals + lax.ppermute(totals, "dp", pairs)
    mine = lax.dynamic_index_in_dim(totals, lax.axis_index("dp"), 0, keepdims=False)
    return (
        output,
        input_grad,
        grad_query,
        grad_key,
        grad_value,
        mine[:count].reshape(heads, slice_q),
        mine[count : 2 * count].reshape(heads, slice_q),
        grad_out,
        mine[2 * count : 2 * count + own_cols],
        grad_gate,
        grad_up,
        grad_down.astype(F32),
        mine[2 * count + own_cols :],
    )


def solution(mesh):
    in_specs = (
        P(("dp", "mp"), None),
        P("dp", "mp"),
        P("dp", "mp"),
        P("dp", "mp"),
        P("mp", "dp"),
        P("mp", "dp"),
        P("mp", "dp"),
        P("dp"),
        P("dp", "mp"),
        P("dp", "mp"),
        P("mp", "dp"),
        P("dp"),
        P(("dp", "mp"), None),
    )
    out_specs = (
        P(("dp", "mp"), None),
        P(("dp", "mp"), None),
        P("dp", "mp"),
        P("dp", "mp"),
        P("dp", "mp"),
        P("mp", "dp"),
        P("mp", "dp"),
        P("mp", "dp"),
        P("dp"),
        P("dp", "mp"),
        P("dp", "mp"),
        P("mp", "dp"),
        P("dp"),
    )

    def body(*args):
        return local(mesh.shape["mp"], mesh.shape["dp"], *args)

    return jax.shard_map(body, mesh=mesh, in_specs=in_specs, out_specs=out_specs, check_vma=False)
```

```python
import functools

import jax
import jax.numpy as jnp
from jax import lax
from jax.experimental import pallas as pl
from jax.experimental.layout import Layout, with_layout_constraint
from jax.experimental.pallas import tpu as pltpu
from jax.sharding import PartitionSpec as P


HD = 128
L = 1024

epsilon = 1e-06
rope_base = 500000.0

BF = jnp.bfloat16
F32 = jnp.float32


def dot_plain(left, right):
    return jnp.dot(left, right, preferred_element_type=F32)


def dot_right_t(left, right):
    return lax.dot_general(left, right, (((1,), (1,)), ((), ())), preferred_element_type=F32)


def dot_left_t(left, right):
    return lax.dot_general(left, right, (((0,), (0,)), ((), ())), preferred_element_type=F32)


def row_major(value):
    return with_layout_constraint(value, Layout(major_to_minor=(0, 1)))


def rope_tables():
    half = HD // 2
    freqs = rope_base ** (-2.0 * jnp.arange(half, dtype=F32) / HD)
    angles = jnp.arange(L).astype(F32)[:, None] * freqs[None, :]
    cosine, sine = jnp.cos(angles), jnp.sin(angles)
    return (
        jnp.concatenate([cosine, cosine], axis=1),
        jnp.concatenate([-sine, sine], axis=1),
    )


def masked_scores(keys, queries, last, rows):
    scores = dot_right_t(keys, queries) * (HD ** (-0.5))
    row = lax.broadcasted_iota(jnp.int32, (rows, rows), 0)
    col = lax.broadcasted_iota(jnp.int32, (rows, rows), 1)
    corner = jnp.where(row <= col, scores[last - rows :, :], -1e30)
    if last == rows:
        return corner
    return jnp.concatenate([scores[: last - rows, :], corner], axis=0)


def forward_kernel(n, rows, me_ref, *refs):
    q_in, k_in, v_in = refs[:n], refs[n : 2 * n], refs[2 * n : 3 * n]
    rate_q, rate_k, gain_q, gain_k, cosine, sine = refs[3 * n : 3 * n + 6]
    attn, q_out, k_out, v_out, lse, turned_v = refs[3 * n + 6 :]
    me = me_ref[0]

    def place(s):
        return pl.multiple_of(lax.rem(me - s + n, n) * rows, rows)

    for s in range(n):
        at = pl.ds(place(s), rows)
        c, d = cosine[at, :], sine[at, :]
        for src, rate, gain, dst in (
            (q_in[s], rate_q, gain_q, q_out),
            (k_in[s], rate_k, gain_k, k_out),
        ):
            normed = src[...] * rate[at, :] * gain[0]
            turned = normed * c + pltpu.roll(normed, HD // 2, 1) * d
            dst[at, :] = turned.astype(BF)
        v_out[at, :] = v_in[s][...].astype(BF)
    turned_v[...] = v_out[...].T
    for piece in range(n):
        first, last = piece * rows, (piece + 1) * rows
        scores = masked_scores(k_out[:last, :], q_out[first:last, :], last, rows)
        peak = jnp.max(scores, axis=0, keepdims=True)
        grown = jnp.exp(scores - peak)
        total = jnp.sum(grown, axis=0, keepdims=True)
        lse[0, :, first:last] = peak + jnp.log(total)
        probs = (grown * (1.0 / total)).astype(BF)
        out = dot_plain(turned_v[:, :last], probs)
        attn[pl.ds(place(piece), rows), :] = out.T.astype(BF)


def backward_kernel(n, rows, me_ref, *refs):
    q_in, k_in, g_in = refs[:n], refs[n : 2 * n], refs[2 * n : 3 * n]
    (rate_q, rate_k, gain_q, gain_k, cosine, sine, q_rot, k_rot, value, lse) = refs[
        3 * n : 3 * n + 10
    ]
    t_q, t_k, d_v, sums, gains = refs[3 * n + 10 : 3 * n + 15]
    grads, turned_k, acc_q, acc_k, acc_v, acc_sums = refs[3 * n + 15 :]
    me = me_ref[0]
    scale = HD ** (-0.5)

    def place(s):
        return pl.multiple_of(lax.rem(me - s + n, n) * rows, rows)

    for s in range(n):
        grads[pl.ds(place(s), rows), :] = g_in[s][...]
    turned_k[...] = k_rot[...].T
    for piece in reversed(range(n)):
        first, last = piece * rows, (piece + 1) * rows
        queries, keys = q_rot[first:last, :], k_rot[:last, :]
        grad = grads[first:last, :]
        scores = masked_scores(keys, queries, last, rows)
        probs = jnp.exp(scores - lse[0, :, first:last])
        d_probs = dot_right_t(value[:last, :], grad)
        delta = jnp.sum(probs * d_probs, axis=0, keepdims=True)
        d_scores = (probs * (d_probs - delta) * scale).astype(BF)
        add_v = dot_plain(probs.astype(BF), grad)
        add_k = dot_plain(d_scores, queries)
        if piece == n - 1:
            acc_v[...] = add_v
            acc_k[...] = add_k
        else:
            acc_v[:last, :] += add_v
            acc_k[:last, :] += add_k
        acc_q[first:last, :] = dot_plain(turned_k[:, :last], d_scores).T
    head = pl.program_id(0)

    @pl.when(head == 0)
    def _():
        acc_sums[...] = jnp.zeros_like(acc_sums)

    for which, (acc, src, rate, gain, out) in enumerate(
        ((acc_q, q_in, rate_q, gain_q, t_q), (acc_k, k_in, rate_k, gain_k, t_k))
    ):
        column = jnp.zeros((1, HD), F32)
        for s in range(n):
            at = pl.ds(place(s), rows)
            grad = acc[at, :]
            normed = grad * cosine[at, :] - pltpu.roll(grad, HD // 2, 1) * sine[at, :]
            hat = src[s][...] * rate[at, :]
            column = column + jnp.sum(normed * hat, axis=0, keepdims=True)
            scaled = normed * gain[0]
            here = slice(s * rows, (s + 1) * rows)
            out[here, :] = scaled
            acc_sums[which, here, :] += scaled * hat
        gains[0, which : which + 1, :] = column
    for s in range(n):
        d_v[s * rows : (s + 1) * rows, :] = acc_v[pl.ds(place(s), rows), :].astype(BF)

    @pl.when(head == pl.num_programs(0) - 1)
    def _():
        for which in range(2):
            sums[which] = jnp.sum(acc_sums[which].T, axis=0, keepdims=True)


def attention_forward(me, pieces, rate_q, rate_k, gain_q, gain_k, cosine, sine):
    n, rows = len(pieces), pieces[0].shape[0]
    heads = gain_q.shape[0]

    def part(offset):
        return [pl.BlockSpec((rows, HD), lambda h, m, o=offset: (0, o * heads + h))] * n

    whole = pl.BlockSpec((L, HD), lambda h, m: (0, 0))
    gain = pl.BlockSpec((1, 1, HD), lambda h, m: (h, 0, 0))
    column = pl.BlockSpec((L, HD), lambda h, m: (0, h))
    low = jax.ShapeDtypeStruct((L, heads * HD), BF)
    return pl.pallas_call(
        functools.partial(forward_kernel, n, rows),
        grid_spec=pltpu.PrefetchScalarGridSpec(
            num_scalar_prefetch=1,
            grid=(heads,),
            in_specs=part(0) + part(1) + part(2) + [whole, whole, gain, gain, whole, whole],
            out_specs=[column] * 4 + [pl.BlockSpec((1, 1, L), lambda h, m: (h, 0, 0))],
            scratch_shapes=[pltpu.VMEM((HD, L), BF)],
        ),
        out_shape=[low] * 4 + [jax.ShapeDtypeStruct((heads, 1, L), F32)],
        compiler_params=pltpu.CompilerParams(vmem_limit_bytes=48 << 20),
        cost_estimate=pl.CostEstimate(
            flops=2 * heads * L * L * HD,
            bytes_accessed=12 * heads * L * HD + 10 * heads * L * HD,
            transcendentals=heads * L * L // 2,
        ),
        name="attention_forward",
    )(
        me,
        *pieces,
        *pieces,
        *pieces,
        rate_q,
        rate_k,
        gain_q[:, None, :],
        gain_k[:, None, :],
        cosine,
        sine,
    )


def attention_backward(
    me, pieces, grads, rate_q, rate_k, gain_q, gain_k, cosine, sine, q_rot, k_rot, value, lse
):
    n, rows = len(pieces), pieces[0].shape[0]
    heads = gain_q.shape[0]

    def part(offset):
        return [pl.BlockSpec((rows, HD), lambda h, m, o=offset: (0, o * heads + h))] * n

    whole = pl.BlockSpec((L, HD), lambda h, m: (0, 0))
    gain = pl.BlockSpec((1, 1, HD), lambda h, m: (h, 0, 0))
    column = pl.BlockSpec((L, HD), lambda h, m: (0, h))
    wide = jax.ShapeDtypeStruct((L, heads * HD), F32)
    return pl.pallas_call(
        functools.partial(backward_kernel, n, rows),
        grid_spec=pltpu.PrefetchScalarGridSpec(
            num_scalar_prefetch=1,
            grid=(heads,),
            in_specs=part(0)
            + part(1)
            + part(0)
            + [whole, whole, gain, gain, whole, whole]
            + [column] * 3
            + [pl.BlockSpec((1, 1, L), lambda h, m: (h, 0, 0))],
            out_specs=[column] * 3
            + [
                pl.BlockSpec((2, 1, L), lambda h, m: (0, 0, 0)),
                pl.BlockSpec((1, 2, HD), lambda h, m: (h, 0, 0)),
            ],
            scratch_shapes=[
                pltpu.VMEM((L, HD), BF),
                pltpu.VMEM((HD, L), BF),
                pltpu.VMEM((L, HD), F32),
                pltpu.VMEM((L, HD), F32),
                pltpu.VMEM((L, HD), F32),
                pltpu.VMEM((2, L, HD), F32),
            ],
        ),
        out_shape=[
            wide,
            wide,
            jax.ShapeDtypeStruct((L, heads * HD), BF),
            jax.ShapeDtypeStruct((2, 1, L), F32),
            jax.ShapeDtypeStruct((heads, 2, HD), F32),
        ],
        compiler_params=pltpu.CompilerParams(vmem_limit_bytes=48 << 20),
        cost_estimate=pl.CostEstimate(
            flops=5 * heads * L * L * HD,
            bytes_accessed=26 * heads * L * HD,
            transcendentals=heads * L * L // 2,
        ),
        name="attention_backward",
    )(
        me,
        *pieces,
        *pieces,
        *grads,
        rate_q,
        rate_k,
        gain_q[:, None, :],
        gain_k[:, None, :],
        cosine,
        sine,
        q_rot,
        k_rot,
        value,
        lse,
    )


def weight_kernel(n, *refs):
    x_in, d_in, a_in = refs[:n], refs[n : 2 * n], refs[2 * n : 3 * n]
    attn, out = refs[3 * n :]
    rows, wide = d_in[0].shape
    one = sum(dot_left_t(x_in[s][...], d_in[s][...]) for s in range(n))
    out[:, :wide] = one.astype(BF)
    two = sum(
        dot_left_t(a_in[s][...], attn[s * rows : (s + 1) * rows, :]) for s in range(n)
    )
    out[:, wide:] = two.astype(BF)


def attention_weights(held_x, d_qkv, held_a, attn):
    n, (rows, wide) = len(held_x), d_qkv[0].shape
    width, narrow = held_x[0].shape[1], attn.shape[1]
    tile = min(256, width)
    step = pl.BlockSpec((rows, tile), lambda i: (0, i))
    once = [pl.BlockSpec((rows, wide), lambda i: (0, 0), pipeline_mode=pl.Buffered(1))]
    return pl.pallas_call(
        functools.partial(weight_kernel, n),
        grid=(width // tile,),
        in_specs=[step] * n
        + once * n
        + [step] * n
        + [pl.BlockSpec((n * rows, narrow), lambda i: (0, 0), pipeline_mode=pl.Buffered(1))],
        out_specs=pl.BlockSpec((tile, wide + narrow), lambda i: (i, 0)),
        out_shape=jax.ShapeDtypeStruct((width, wide + narrow), BF),
        compiler_params=pltpu.CompilerParams(vmem_limit_bytes=40 << 20),
        cost_estimate=pl.CostEstimate(
            flops=2 * n * rows * width * (wide + narrow),
            bytes_accessed=2 * (width + n * rows) * (wide + narrow) + 4 * n * rows * width,
            transcendentals=0,
        ),
        name="attention_weights",
    )(*held_x, *d_qkv, *held_a, attn)


def half_kernel(n, *refs):
    x_in, d_in, out = refs[:n], refs[n : 2 * n], refs[-1]
    out[...] = sum(dot_left_t(x_in[s][...], d_in[s][...]) for s in range(n)).astype(BF)


def half_weights(held, grads, which, buffer=None):
    n, (rows, wide) = len(held), grads[0].shape
    width = held[0].shape[1]
    tile = min(256, width)
    step = pl.BlockSpec((rows, tile), lambda i: (0, i))
    once = pl.BlockSpec((rows, wide), lambda i: (0, 0), pipeline_mode=pl.Buffered(1))
    rest = () if buffer is None else (buffer,)
    return pl.pallas_call(
        functools.partial(half_kernel, n),
        grid=(width // tile,),
        in_specs=[step] * n + [once] * n + [pl.BlockSpec(memory_space=pl.ANY)] * len(rest),
        out_specs=pl.BlockSpec((tile, wide), lambda i: (i, which)),
        out_shape=jax.ShapeDtypeStruct((width, 2 * wide), BF),
        input_output_aliases={2 * n: 0} if rest else {},
        compiler_params=pltpu.CompilerParams(vmem_limit_bytes=40 << 20),
        cost_estimate=pl.CostEstimate(
            flops=2 * n * rows * width * wide,
            bytes_accessed=2 * (width * wide + n * rows * (wide + width)),
            transcendentals=0,
        ),
    )(*held, *grads, *rest)


def local(
    n,
    groups,
    inputs,
    w_query,
    w_key,
    w_value,
    q_gain,
    k_gain,
    w_out,
    attn_gain,
    w_gate,
    w_up,
    w_down,
    mlp_gain,
    cotangent,
):
    rows, width = inputs.shape
    heads, slice_q = q_gain.shape
    head_cols = heads * HD
    units = w_gate.shape[1]
    me = lax.axis_index("mp").astype(jnp.int32)
    me_ref = me.reshape(1)
    ring = [(i, (i + 1) % n) for i in range(n)]

    def shift(value):
        return lax.ppermute(value, "mp", ring)

    def sum_all(value):
        total = value
        for k in range(1, n):
            total = total + lax.ppermute(value, "mp", [(i, (i + k) % n) for i in range(n)])
        return total

    def reorder(stacked):
        turned = stacked[::-1]
        return lax.dynamic_slice_in_dim(
            jnp.concatenate([turned, turned], axis=0), n - 1 - me, n, axis=0
        )

    def gather_ring(own, first=1, last=n - 1, after={}):
        held = [own]
        for s in range(first, last + 1):
            sent = held[-1]
            if s in after:
                sent = lax.optimization_barrier((sent, after[s]))[0]
            held.append(shift(sent))
        return held

    def scatter_ring(partial_of, after={}):
        running = None
        for s in range(1, n):
            term = partial_of(s)
            if running is not None:
                term = term + running.astype(F32)
            term = term.astype(BF)
            if s in after:
                term = lax.optimization_barrier((term, after[s]))[0]
            running = shift(term)
        return partial_of(0) + running.astype(F32)

    w_attn = lax.all_gather(
        row_major(jnp.concatenate([w_query, w_key, w_value, row_major(w_out.T)], axis=1)),
        "dp",
        axis=0,
        tiled=True,
    )
    w_qkv = w_attn[:, : 3 * head_cols]
    out_t = w_attn[:, 3 * head_cols :]
    small = jnp.concatenate(
        [q_gain.reshape(-1), k_gain.reshape(-1), attn_gain, mlp_gain], axis=0
    )
    small = lax.all_gather(small, "dp", axis=0, tiled=False).astype(F32)
    count = heads * slice_q
    gain_q = small[:, :count].reshape(groups, heads, slice_q).transpose(1, 0, 2).reshape(heads, HD)
    gain_k = (
        small[:, count : 2 * count]
        .reshape(groups, heads, slice_q)
        .transpose(1, 0, 2)
        .reshape(heads, HD)
    )
    own_cols = attn_gain.shape[0]
    gain_a = small[:, 2 * count : 2 * count + own_cols].reshape(width)
    gain_m = small[:, 2 * count + own_cols :].reshape(width)
    shard_gate_up = jnp.concatenate([w_gate, w_up], axis=1)
    full_gate_up = lax.all_gather(shard_gate_up, "dp", axis=0, tiled=True)
    full_gate, full_up = lax.optimization_barrier(
        (full_gate_up[:, :units], full_gate_up[:, units:])
    )
    full_down = lax.all_gather(w_down, "dp", axis=1, tiled=True)
    cosine, sine = rope_tables()

    held_x = gather_ring(inputs)
    pieces = []
    for x in held_x:
        pieces.append(dot_plain(x, w_qkv))
    squares = jnp.stack(
        [
            jnp.stack(
                [
                    jnp.sum(jnp.square(p[:, :head_cols]), axis=1),
                    jnp.sum(jnp.square(p[:, head_cols : 2 * head_cols]), axis=1),
                ]
            )
            for p in pieces
        ]
    )
    squares = sum_all(reorder(squares))
    rates = lax.rsqrt(squares / width + epsilon)
    rate_q = jnp.broadcast_to(rates[:, 0].reshape(L, 1), (L, HD))
    rate_k = jnp.broadcast_to(rates[:, 1].reshape(L, 1), (L, HD))
    attn, q_rot, k_rot, value, lse = attention_forward(
        me_ref, pieces, rate_q, rate_k, gain_q, gain_k, cosine, sine
    )
    attn_proj = scatter_ring(lambda s: dot_right_t(attn[s * rows : (s + 1) * rows], out_t))
    rate_a = lax.rsqrt(jnp.mean(attn_proj * attn_proj, axis=1, keepdims=True) + epsilon)
    hat_a = attn_proj * rate_a
    resid = inputs.astype(F32) + hat_a * gain_a
    resid_low = resid.astype(BF)

    held_r = gather_ring(resid_low)
    gates, ups, hiddens = [], [], []
    for r in held_r:
        gate = dot_plain(r, full_gate)
        up = dot_plain(r, full_up)
        gates.append(gate)
        ups.append(up)
        hiddens.append((gate * jax.nn.sigmoid(gate) * up).astype(BF))
    mlp_proj = scatter_ring(lambda s: dot_plain(hiddens[s], full_down))
    rate_m = lax.rsqrt(jnp.mean(mlp_proj * mlp_proj, axis=1, keepdims=True) + epsilon)
    hat_m = mlp_proj * rate_m
    output = resid + hat_m * gain_m

    upstream = cotangent.astype(F32)
    grad_gain_m = jnp.sum(upstream * hat_m, axis=0)
    scaled_m = upstream * gain_m
    d_mlp = (
        rate_m * (scaled_m - hat_m * jnp.mean(scaled_m * hat_m, axis=1, keepdims=True))
    ).astype(BF)
    held_m = gather_ring(d_mlp)
    d_gates, d_ups = [], []
    for s in range(n):
        gate, up = gates[s], ups[s]
        sigma = jax.nn.sigmoid(gate)
        d_hidden = dot_right_t(held_m[s], full_down)
        d_gates.append((d_hidden * up * sigma * (1.0 + gate * (1.0 - sigma))).astype(BF))
        d_ups.append((d_hidden * (gate * sigma)).astype(BF))
    down = dot_left_t(jnp.concatenate(hiddens, axis=0), jnp.concatenate(held_m, axis=0)).astype(BF)
    d_resid = upstream + scatter_ring(
        lambda s: dot_right_t(d_gates[s], full_gate) + dot_right_t(d_ups[s], full_up),
        {1: held_m[-1]},
    )
    grad_down = lax.psum_scatter(down, "dp", scatter_dimension=1, tiled=True)
    gate_up = half_weights(held_r, d_gates, 0)
    gate_up = half_weights(held_r, d_ups, 1, gate_up)

    grad_gain_a = jnp.sum(d_resid * hat_a, axis=0)
    scaled_a = d_resid * gain_a
    d_attn_proj = (
        rate_a * (scaled_a - hat_a * jnp.mean(scaled_a * hat_a, axis=1, keepdims=True))
    ).astype(BF)
    held_a = gather_ring(d_attn_proj, after={n - 1: grad_down})
    grad_gate_up = lax.psum_scatter(gate_up, "dp", scatter_dimension=0, tiled=True)
    d_attn = [dot_plain(a, out_t).astype(BF) for a in held_a]
    t_q, t_k, d_value, sums, head_gains = attention_backward(
        me_ref,
        pieces,
        d_attn,
        rate_q,
        rate_k,
        gain_q,
        gain_k,
        cosine,
        sine,
        q_rot,
        k_rot,
        value,
        lse,
    )
    sums = reorder(sums[:, 0, :].reshape(2, n, rows).transpose(1, 0, 2))
    sums = sum_all(sums)
    back = reorder(jnp.concatenate([rates, sums / width], axis=1))
    d_qkv = []
    for s in range(n):
        at = slice(s * rows, (s + 1) * rows)
        parts = []
        for which, t in enumerate((t_q, t_k)):
            rate = back[s, which][:, None]
            raw = pieces[s][:, which * head_cols : (which + 1) * head_cols]
            parts.append((rate * (t[at] - raw * (rate * back[s, 2 + which][:, None]))).astype(BF))
        parts.append(d_value[at])
        d_qkv.append(jnp.concatenate(parts, axis=1))
    dw_attn = attention_weights(held_x, d_qkv, held_a, attn)
    grad_attn = lax.psum_scatter(dw_attn, "dp", scatter_dimension=0, tiled=True)
    input_grad = d_resid + scatter_ring(
        lambda s: dot_right_t(d_qkv[s], w_qkv), {n - 1: grad_gate_up}
    )

    grad_attn, input_grad = lax.optimization_barrier((grad_attn, input_grad))
    grad_query = grad_attn[:, :head_cols].astype(F32)
    grad_key = grad_attn[:, head_cols : 2 * head_cols].astype(F32)
    grad_value = grad_attn[:, 2 * head_cols : 3 * head_cols].astype(F32)
    grad_out = grad_attn[:, 3 * head_cols :].astype(F32).T
    grad_gate = grad_gate_up[:, :units].astype(F32)
    grad_up = grad_gate_up[:, units:].astype(F32)

    post = sum_all(jnp.stack([grad_gain_a, grad_gain_m]))
    post = post.reshape(2, groups, own_cols).transpose(1, 0, 2).reshape(groups, 2 * own_cols)
    own = head_gains.transpose(1, 0, 2).reshape(2, heads, groups, slice_q)
    own = own.transpose(2, 0, 1, 3).reshape(groups, 2 * count)
    totals = jnp.concatenate([own, post], axis=1)
    if groups & (groups - 1):
        totals = lax.psum(totals, "dp")
    else:
        for k in range(groups.bit_length() - 1):
            pairs = [(i, i ^ (1 << k)) for i in range(groups)]
            totals = totals + lax.ppermute(totals, "dp", pairs)
    mine = lax.dynamic_index_in_dim(totals, lax.axis_index("dp"), 0, keepdims=False)
    return (
        output,
        input_grad,
        grad_query,
        grad_key,
        grad_value,
        mine[:count].reshape(heads, slice_q),
        mine[count : 2 * count].reshape(heads, slice_q),
        grad_out,
        mine[2 * count : 2 * count + own_cols],
        grad_gate,
        grad_up,
        grad_down.astype(F32),
        mine[2 * count + own_cols :],
    )


def solution(mesh):
    in_specs = (
        P(("dp", "mp"), None),
        P("dp", "mp"),
        P("dp", "mp"),
        P("dp", "mp"),
        P("mp", "dp"),
        P("mp", "dp"),
        P("mp", "dp"),
        P("dp"),
        P("dp", "mp"),
        P("dp", "mp"),
        P("mp", "dp"),
        P("dp"),
        P(("dp", "mp"), None),
    )
    out_specs = (
        P(("dp", "mp"), None),
        P(("dp", "mp"), None),
        P("dp", "mp"),
        P("dp", "mp"),
        P("dp", "mp"),
        P("mp", "dp"),
        P("mp", "dp"),
        P("mp", "dp"),
        P("dp"),
        P("dp", "mp"),
        P("dp", "mp"),
        P("mp", "dp"),
        P("dp"),
    )

    def body(*args):
        return local(mesh.shape["mp"], mesh.shape["dp"], *args)

    return jax.shard_map(body, mesh=mesh, in_specs=in_specs, out_specs=out_specs, check_vma=False)
```

```python
import functools

import jax
import jax.numpy as jnp
from jax import lax
from jax.experimental import pallas as pl
from jax.experimental.layout import Layout, with_layout_constraint
from jax.experimental.pallas import tpu as pltpu
from jax.sharding import PartitionSpec as P


HD = 128
L = 1024

epsilon = 1e-06
rope_base = 500000.0

BF = jnp.bfloat16
F32 = jnp.float32


def dot_plain(left, right):
    return jnp.dot(left, right, preferred_element_type=F32)


def dot_right_t(left, right):
    return lax.dot_general(left, right, (((1,), (1,)), ((), ())), preferred_element_type=F32)


def dot_left_t(left, right):
    return lax.dot_general(left, right, (((0,), (0,)), ((), ())), preferred_element_type=F32)


def row_major(value):
    return with_layout_constraint(value, Layout(major_to_minor=(0, 1)))


def rope_tables():
    half = HD // 2
    freqs = rope_base ** (-2.0 * jnp.arange(half, dtype=F32) / HD)
    angles = jnp.arange(L).astype(F32)[:, None] * freqs[None, :]
    cosine, sine = jnp.cos(angles), jnp.sin(angles)
    return (
        jnp.concatenate([cosine, cosine], axis=1),
        jnp.concatenate([-sine, sine], axis=1),
    )


def masked_scores(keys, queries, last, rows):
    scores = dot_right_t(keys, queries) * (HD ** (-0.5))
    row = lax.broadcasted_iota(jnp.int32, (rows, rows), 0)
    col = lax.broadcasted_iota(jnp.int32, (rows, rows), 1)
    corner = jnp.where(row <= col, scores[last - rows :, :], -1e30)
    if last == rows:
        return corner
    return jnp.concatenate([scores[: last - rows, :], corner], axis=0)


def forward_kernel(n, rows, me_ref, *refs):
    q_in, k_in, v_in = refs[:n], refs[n : 2 * n], refs[2 * n : 3 * n]
    rate_q, rate_k, gain_q, gain_k, cosine, sine = refs[3 * n : 3 * n + 6]
    attn, q_out, k_out, v_out, lse, turned_v = refs[3 * n + 6 :]
    me = me_ref[0]

    def place(s):
        return pl.multiple_of(lax.rem(me - s + n, n) * rows, rows)

    for s in range(n):
        at = pl.ds(place(s), rows)
        c, d = cosine[at, :], sine[at, :]
        for src, rate, gain, dst in (
            (q_in[s], rate_q, gain_q, q_out),
            (k_in[s], rate_k, gain_k, k_out),
        ):
            normed = src[...] * rate[at, :] * gain[0]
            turned = normed * c + pltpu.roll(normed, HD // 2, 1) * d
            dst[at, :] = turned.astype(BF)
        v_out[at, :] = v_in[s][...].astype(BF)
    turned_v[...] = v_out[...].T
    for piece in range(n):
        first, last = piece * rows, (piece + 1) * rows
        scores = masked_scores(k_out[:last, :], q_out[first:last, :], last, rows)
        peak = jnp.max(scores, axis=0, keepdims=True)
        grown = jnp.exp(scores - peak)
        total = jnp.sum(grown, axis=0, keepdims=True)
        lse[0, :, first:last] = peak + jnp.log(total)
        probs = (grown * (1.0 / total)).astype(BF)
        out = dot_plain(turned_v[:, :last], probs)
        attn[pl.ds(place(piece), rows), :] = out.T.astype(BF)


def backward_kernel(n, rows, me_ref, *refs):
    q_in, k_in, g_in = refs[:n], refs[n : 2 * n], refs[2 * n : 3 * n]
    (rate_q, rate_k, gain_q, gain_k, cosine, sine, q_rot, k_rot, value, lse) = refs[
        3 * n : 3 * n + 10
    ]
    t_q, t_k, d_v, sums, gains = refs[3 * n + 10 : 3 * n + 15]
    grads, turned_k, acc_q, acc_k, acc_v, acc_sums = refs[3 * n + 15 :]
    me = me_ref[0]
    scale = HD ** (-0.5)

    def place(s):
        return pl.multiple_of(lax.rem(me - s + n, n) * rows, rows)

    for s in range(n):
        grads[pl.ds(place(s), rows), :] = g_in[s][...]
    turned_k[...] = k_rot[...].T
    for piece in reversed(range(n)):
        first, last = piece * rows, (piece + 1) * rows
        queries, keys = q_rot[first:last, :], k_rot[:last, :]
        grad = grads[first:last, :]
        scores = masked_scores(keys, queries, last, rows)
        probs = jnp.exp(scores - lse[0, :, first:last])
        d_probs = dot_right_t(value[:last, :], grad)
        delta = jnp.sum(probs * d_probs, axis=0, keepdims=True)
        d_scores = (probs * (d_probs - delta) * scale).astype(BF)
        add_v = dot_plain(probs.astype(BF), grad)
        add_k = dot_plain(d_scores, queries)
        if piece == n - 1:
            acc_v[...] = add_v
            acc_k[...] = add_k
        else:
            acc_v[:last, :] += add_v
            acc_k[:last, :] += add_k
        acc_q[first:last, :] = dot_plain(turned_k[:, :last], d_scores).T
    head = pl.program_id(0)

    @pl.when(head == 0)
    def _():
        acc_sums[...] = jnp.zeros_like(acc_sums)

    for which, (acc, src, rate, gain, out) in enumerate(
        ((acc_q, q_in, rate_q, gain_q, t_q), (acc_k, k_in, rate_k, gain_k, t_k))
    ):
        column = jnp.zeros((1, HD), F32)
        for s in range(n):
            at = pl.ds(place(s), rows)
            grad = acc[at, :]
            normed = grad * cosine[at, :] - pltpu.roll(grad, HD // 2, 1) * sine[at, :]
            hat = src[s][...] * rate[at, :]
            column = column + jnp.sum(normed * hat, axis=0, keepdims=True)
            scaled = normed * gain[0]
            here = slice(s * rows, (s + 1) * rows)
            out[here, :] = scaled
            acc_sums[which, here, :] += scaled * hat
        gains[0, which : which + 1, :] = column
    for s in range(n):
        d_v[s * rows : (s + 1) * rows, :] = acc_v[pl.ds(place(s), rows), :].astype(BF)

    @pl.when(head == pl.num_programs(0) - 1)
    def _():
        for which in range(2):
            sums[which] = jnp.sum(acc_sums[which].T, axis=0, keepdims=True)


def attention_forward(me, pieces, rate_q, rate_k, gain_q, gain_k, cosine, sine):
    n, rows = len(pieces), pieces[0].shape[0]
    heads = gain_q.shape[0]

    def part(offset):
        return [pl.BlockSpec((rows, HD), lambda h, m, o=offset: (0, o * heads + h))] * n

    whole = pl.BlockSpec((L, HD), lambda h, m: (0, 0))
    gain = pl.BlockSpec((1, 1, HD), lambda h, m: (h, 0, 0))
    column = pl.BlockSpec((L, HD), lambda h, m: (0, h))
    low = jax.ShapeDtypeStruct((L, heads * HD), BF)
    return pl.pallas_call(
        functools.partial(forward_kernel, n, rows),
        grid_spec=pltpu.PrefetchScalarGridSpec(
            num_scalar_prefetch=1,
            grid=(heads,),
            in_specs=part(0) + part(1) + part(2) + [whole, whole, gain, gain, whole, whole],
            out_specs=[column] * 4 + [pl.BlockSpec((1, 1, L), lambda h, m: (h, 0, 0))],
            scratch_shapes=[pltpu.VMEM((HD, L), BF)],
        ),
        out_shape=[low] * 4 + [jax.ShapeDtypeStruct((heads, 1, L), F32)],
        compiler_params=pltpu.CompilerParams(vmem_limit_bytes=48 << 20),
        cost_estimate=pl.CostEstimate(
            flops=2 * heads * L * L * HD,
            bytes_accessed=12 * heads * L * HD + 10 * heads * L * HD,
            transcendentals=heads * L * L // 2,
        ),
        name="attention_forward",
    )(
        me,
        *pieces,
        *pieces,
        *pieces,
        rate_q,
        rate_k,
        gain_q[:, None, :],
        gain_k[:, None, :],
        cosine,
        sine,
    )


def attention_backward(
    me, pieces, grads, rate_q, rate_k, gain_q, gain_k, cosine, sine, q_rot, k_rot, value, lse
):
    n, rows = len(pieces), pieces[0].shape[0]
    heads = gain_q.shape[0]

    def part(offset):
        return [pl.BlockSpec((rows, HD), lambda h, m, o=offset: (0, o * heads + h))] * n

    whole = pl.BlockSpec((L, HD), lambda h, m: (0, 0))
    gain = pl.BlockSpec((1, 1, HD), lambda h, m: (h, 0, 0))
    column = pl.BlockSpec((L, HD), lambda h, m: (0, h))
    wide = jax.ShapeDtypeStruct((L, heads * HD), F32)
    return pl.pallas_call(
        functools.partial(backward_kernel, n, rows),
        grid_spec=pltpu.PrefetchScalarGridSpec(
            num_scalar_prefetch=1,
            grid=(heads,),
            in_specs=part(0)
            + part(1)
            + part(0)
            + [whole, whole, gain, gain, whole, whole]
            + [column] * 3
            + [pl.BlockSpec((1, 1, L), lambda h, m: (h, 0, 0))],
            out_specs=[column] * 3
            + [
                pl.BlockSpec((2, 1, L), lambda h, m: (0, 0, 0)),
                pl.BlockSpec((1, 2, HD), lambda h, m: (h, 0, 0)),
            ],
            scratch_shapes=[
                pltpu.VMEM((L, HD), BF),
                pltpu.VMEM((HD, L), BF),
                pltpu.VMEM((L, HD), F32),
                pltpu.VMEM((L, HD), F32),
                pltpu.VMEM((L, HD), F32),
                pltpu.VMEM((2, L, HD), F32),
            ],
        ),
        out_shape=[
            wide,
            wide,
            jax.ShapeDtypeStruct((L, heads * HD), BF),
            jax.ShapeDtypeStruct((2, 1, L), F32),
            jax.ShapeDtypeStruct((heads, 2, HD), F32),
        ],
        compiler_params=pltpu.CompilerParams(vmem_limit_bytes=48 << 20),
        cost_estimate=pl.CostEstimate(
            flops=5 * heads * L * L * HD,
            bytes_accessed=26 * heads * L * HD,
            transcendentals=heads * L * L // 2,
        ),
        name="attention_backward",
    )(
        me,
        *pieces,
        *pieces,
        *grads,
        rate_q,
        rate_k,
        gain_q[:, None, :],
        gain_k[:, None, :],
        cosine,
        sine,
        q_rot,
        k_rot,
        value,
        lse,
    )


def weight_kernel(n, *refs):
    x_in, d_in, a_in = refs[:n], refs[n : 2 * n], refs[2 * n : 3 * n]
    attn, first, second = refs[3 * n :]
    rows = d_in[0].shape[0]
    cut, narrow = first.shape[1], attn.shape[1]
    one = sum(dot_left_t(x_in[s][...], d_in[s][...]) for s in range(n))
    first[...] = one[:, :cut].astype(BF)
    second[:, : second.shape[1] - narrow] = one[:, cut:].astype(BF)
    two = sum(
        dot_left_t(a_in[s][...], attn[s * rows : (s + 1) * rows, :]) for s in range(n)
    )
    second[:, second.shape[1] - narrow :] = two.astype(BF)


def attention_weights(held_x, d_qkv, held_a, attn):
    n, (rows, wide) = len(held_x), d_qkv[0].shape
    width, narrow = held_x[0].shape[1], attn.shape[1]
    tile = min(256, width)
    step = pl.BlockSpec((rows, tile), lambda i: (0, i))
    once = [pl.BlockSpec((rows, wide), lambda i: (0, 0), pipeline_mode=pl.Buffered(1))]
    return pl.pallas_call(
        functools.partial(weight_kernel, n),
        grid=(width // tile,),
        in_specs=[step] * n
        + once * n
        + [step] * n
        + [pl.BlockSpec((n * rows, narrow), lambda i: (0, 0), pipeline_mode=pl.Buffered(1))],
        out_specs=[pl.BlockSpec((tile, 2 * narrow), lambda i: (i, 0))] * 2,
        out_shape=[jax.ShapeDtypeStruct((width, 2 * narrow), BF)] * 2,
        compiler_params=pltpu.CompilerParams(vmem_limit_bytes=40 << 20),
        cost_estimate=pl.CostEstimate(
            flops=2 * n * rows * width * (wide + narrow),
            bytes_accessed=2 * (width + n * rows) * (wide + narrow) + 4 * n * rows * width,
            transcendentals=0,
        ),
        name="attention_weights",
    )(*held_x, *d_qkv, *held_a, attn)


def half_kernel(n, *refs):
    x_in, d_in, out = refs[:n], refs[n : 2 * n], refs[-1]
    out[...] = sum(dot_left_t(x_in[s][...], d_in[s][...]) for s in range(n)).astype(BF)


def half_weights(held, grads, which, buffer=None):
    n, (rows, wide) = len(held), grads[0].shape
    width = held[0].shape[1]
    tile = min(256, width)
    step = pl.BlockSpec((rows, tile), lambda i: (0, i))
    once = pl.BlockSpec((rows, wide), lambda i: (0, 0), pipeline_mode=pl.Buffered(1))
    rest = () if buffer is None else (buffer,)
    return pl.pallas_call(
        functools.partial(half_kernel, n),
        grid=(width // tile,),
        in_specs=[step] * n + [once] * n + [pl.BlockSpec(memory_space=pl.ANY)] * len(rest),
        out_specs=pl.BlockSpec((tile, wide), lambda i: (i, which)),
        out_shape=jax.ShapeDtypeStruct((width, 2 * wide), BF),
        input_output_aliases={2 * n: 0} if rest else {},
        compiler_params=pltpu.CompilerParams(vmem_limit_bytes=40 << 20),
        cost_estimate=pl.CostEstimate(
            flops=2 * n * rows * width * wide,
            bytes_accessed=2 * (width * wide + n * rows * (wide + width)),
            transcendentals=0,
        ),
    )(*held, *grads, *rest)


def local(
    n,
    groups,
    inputs,
    w_query,
    w_key,
    w_value,
    q_gain,
    k_gain,
    w_out,
    attn_gain,
    w_gate,
    w_up,
    w_down,
    mlp_gain,
    cotangent,
):
    rows, width = inputs.shape
    heads, slice_q = q_gain.shape
    head_cols = heads * HD
    units = w_gate.shape[1]
    me = lax.axis_index("mp").astype(jnp.int32)
    me_ref = me.reshape(1)
    ring = [(i, (i + 1) % n) for i in range(n)]

    def shift(value):
        return lax.ppermute(value, "mp", ring)

    def sum_all(value):
        total = value
        for k in range(1, n):
            total = total + lax.ppermute(value, "mp", [(i, (i + k) % n) for i in range(n)])
        return total

    def halve(whole):
        if groups & (groups - 1):
            return lax.psum_scatter(whole, "dp", scatter_dimension=0, tiled=True).astype(F32)
        place = lax.axis_index("dp")
        left = whole.reshape(groups, whole.shape[0] // groups, whole.shape[1])
        for k in range(groups.bit_length() - 1):
            bit = (place >> k) & 1
            paired = left.reshape(left.shape[0] // 2, 2, *left.shape[1:])
            kept = lax.dynamic_index_in_dim(paired, bit, 1, keepdims=False)
            sent = lax.dynamic_index_in_dim(paired, 1 - bit, 1, keepdims=False)
            got = lax.ppermute(sent.astype(BF), "dp", [(i, i ^ (1 << k)) for i in range(groups)])
            left = kept.astype(F32) + got.astype(F32)
            if left.shape[0] > 1:
                left = left.astype(BF)
        return left[0]

    def reorder(stacked):
        turned = stacked[::-1]
        return lax.dynamic_slice_in_dim(
            jnp.concatenate([turned, turned], axis=0), n - 1 - me, n, axis=0
        )

    def gather_ring(own, first=1, last=n - 1, after={}):
        held = [own]
        for s in range(first, last + 1):
            sent = held[-1]
            if s in after:
                sent = lax.optimization_barrier((sent, after[s]))[0]
            held.append(shift(sent))
        return held

    def scatter_ring(partial_of, after={}):
        running = None
        for s in range(1, n):
            term = partial_of(s)
            if running is not None:
                term = term + running.astype(F32)
            term = term.astype(BF)
            if s in after:
                term = lax.optimization_barrier((term, after[s]))[0]
            running = shift(term)
        return partial_of(0) + running.astype(F32)

    w_attn = lax.all_gather(
        row_major(jnp.concatenate([w_query, w_key, w_value, row_major(w_out.T)], axis=1)),
        "dp",
        axis=0,
        tiled=True,
    )
    w_qkv = w_attn[:, : 3 * head_cols]
    out_t = w_attn[:, 3 * head_cols :]
    small = jnp.concatenate(
        [q_gain.reshape(-1), k_gain.reshape(-1), attn_gain, mlp_gain], axis=0
    )
    small = lax.all_gather(small, "dp", axis=0, tiled=False).astype(F32)
    count = heads * slice_q
    gain_q = small[:, :count].reshape(groups, heads, slice_q).transpose(1, 0, 2).reshape(heads, HD)
    gain_k = (
        small[:, count : 2 * count]
        .reshape(groups, heads, slice_q)
        .transpose(1, 0, 2)
        .reshape(heads, HD)
    )
    own_cols = attn_gain.shape[0]
    gain_a = small[:, 2 * count : 2 * count + own_cols].reshape(width)
    gain_m = small[:, 2 * count + own_cols :].reshape(width)
    shard_gate_up = jnp.concatenate([w_gate, w_up], axis=1)
    full_gate_up = lax.all_gather(shard_gate_up, "dp", axis=0, tiled=True)
    full_gate, full_up = lax.optimization_barrier(
        (full_gate_up[:, :units], full_gate_up[:, units:])
    )
    full_down = lax.all_gather(w_down, "dp", axis=1, tiled=True)
    cosine, sine = rope_tables()

    held_x = gather_ring(inputs)
    pieces = []
    for x in held_x:
        pieces.append(dot_plain(x, w_qkv))
    squares = jnp.stack(
        [
            jnp.stack(
                [
                    jnp.sum(jnp.square(p[:, :head_cols]), axis=1),
                    jnp.sum(jnp.square(p[:, head_cols : 2 * head_cols]), axis=1),
                ]
            )
            for p in pieces
        ]
    )
    squares = sum_all(reorder(squares))
    rates = lax.rsqrt(squares / width + epsilon)
    rate_q = jnp.broadcast_to(rates[:, 0].reshape(L, 1), (L, HD))
    rate_k = jnp.broadcast_to(rates[:, 1].reshape(L, 1), (L, HD))
    attn, q_rot, k_rot, value, lse = attention_forward(
        me_ref, pieces, rate_q, rate_k, gain_q, gain_k, cosine, sine
    )
    attn_proj = scatter_ring(lambda s: dot_right_t(attn[s * rows : (s + 1) * rows], out_t))
    rate_a = lax.rsqrt(jnp.mean(attn_proj * attn_proj, axis=1, keepdims=True) + epsilon)
    hat_a = attn_proj * rate_a
    resid = inputs.astype(F32) + hat_a * gain_a
    resid_low = resid.astype(BF)

    held_r = gather_ring(resid_low)
    gates, ups, hiddens = [], [], []
    for r in held_r:
        gate = dot_plain(r, full_gate)
        up = dot_plain(r, full_up)
        gates.append(gate)
        ups.append(up)
        hiddens.append((gate * jax.nn.sigmoid(gate) * up).astype(BF))
    mlp_proj = scatter_ring(lambda s: dot_plain(hiddens[s], full_down))
    rate_m = lax.rsqrt(jnp.mean(mlp_proj * mlp_proj, axis=1, keepdims=True) + epsilon)
    hat_m = mlp_proj * rate_m
    output = resid + hat_m * gain_m

    upstream = cotangent.astype(F32)
    grad_gain_m = jnp.sum(upstream * hat_m, axis=0)
    scaled_m = upstream * gain_m
    d_mlp = (
        rate_m * (scaled_m - hat_m * jnp.mean(scaled_m * hat_m, axis=1, keepdims=True))
    ).astype(BF)
    held_m = gather_ring(d_mlp)
    d_gates, d_ups = [], []
    for s in range(n):
        gate, up = gates[s], ups[s]
        sigma = jax.nn.sigmoid(gate)
        d_hidden = dot_right_t(held_m[s], full_down)
        d_gates.append((d_hidden * up * sigma * (1.0 + gate * (1.0 - sigma))).astype(BF))
        d_ups.append((d_hidden * (gate * sigma)).astype(BF))
    down = dot_left_t(jnp.concatenate(hiddens, axis=0), jnp.concatenate(held_m, axis=0)).astype(BF)
    d_resid = upstream + scatter_ring(
        lambda s: dot_right_t(d_gates[s], full_gate) + dot_right_t(d_ups[s], full_up),
        {1: held_m[-1]},
    )
    grad_down = lax.psum_scatter(down, "dp", scatter_dimension=1, tiled=True)
    gate_up = half_weights(held_r, d_gates, 0)
    gate_up = half_weights(held_r, d_ups, 1, gate_up)

    grad_gain_a = jnp.sum(d_resid * hat_a, axis=0)
    scaled_a = d_resid * gain_a
    d_attn_proj = (
        rate_a * (scaled_a - hat_a * jnp.mean(scaled_a * hat_a, axis=1, keepdims=True))
    ).astype(BF)
    held_a = gather_ring(d_attn_proj, after={n - 1: grad_down})
    grad_gate_up = lax.psum_scatter(gate_up, "dp", scatter_dimension=0, tiled=True)
    d_attn = [dot_plain(a, out_t).astype(BF) for a in held_a]
    t_q, t_k, d_value, sums, head_gains = attention_backward(
        me_ref,
        pieces,
        d_attn,
        rate_q,
        rate_k,
        gain_q,
        gain_k,
        cosine,
        sine,
        q_rot,
        k_rot,
        value,
        lse,
    )
    sums = reorder(sums[:, 0, :].reshape(2, n, rows).transpose(1, 0, 2))
    sums = sum_all(sums)
    back = reorder(jnp.concatenate([rates, sums / width], axis=1))
    d_qkv = []
    for s in range(n):
        at = slice(s * rows, (s + 1) * rows)
        parts = []
        for which, t in enumerate((t_q, t_k)):
            rate = back[s, which][:, None]
            raw = pieces[s][:, which * head_cols : (which + 1) * head_cols]
            parts.append((rate * (t[at] - raw * (rate * back[s, 2 + which][:, None]))).astype(BF))
        parts.append(d_value[at])
        d_qkv.append(jnp.concatenate(parts, axis=1))
    dw_attn, dw_rest = attention_weights(held_x, d_qkv, held_a, attn)
    grad_attn = lax.psum_scatter(dw_attn, "dp", scatter_dimension=0, tiled=True)
    input_grad = d_resid + scatter_ring(
        lambda s: dot_right_t(d_qkv[s], w_qkv), {n - 1: grad_gate_up}
    )

    grad_rest = halve(dw_rest)
    grad_attn, input_grad = lax.optimization_barrier((grad_attn, input_grad))
    grad_query = grad_attn[:, :head_cols].astype(F32)
    grad_key = grad_attn[:, head_cols : 2 * head_cols].astype(F32)
    grad_value = grad_rest[:, :head_cols]
    grad_out = grad_rest[:, head_cols:].T
    grad_gate = grad_gate_up[:, :units].astype(F32)
    grad_up = grad_gate_up[:, units:].astype(F32)

    post = sum_all(jnp.stack([grad_gain_a, grad_gain_m]))
    post = post.reshape(2, groups, own_cols).transpose(1, 0, 2).reshape(groups, 2 * own_cols)
    own = head_gains.transpose(1, 0, 2).reshape(2, heads, groups, slice_q)
    own = own.transpose(2, 0, 1, 3).reshape(groups, 2 * count)
    totals = jnp.concatenate([own, post], axis=1)
    if groups & (groups - 1):
        totals = lax.psum(totals, "dp")
    else:
        for k in range(groups.bit_length() - 1):
            pairs = [(i, i ^ (1 << k)) for i in range(groups)]
            totals = totals + lax.ppermute(totals, "dp", pairs)
    mine = lax.dynamic_index_in_dim(totals, lax.axis_index("dp"), 0, keepdims=False)
    return (
        output,
        input_grad,
        grad_query,
        grad_key,
        grad_value,
        mine[:count].reshape(heads, slice_q),
        mine[count : 2 * count].reshape(heads, slice_q),
        grad_out,
        mine[2 * count : 2 * count + own_cols],
        grad_gate,
        grad_up,
        grad_down.astype(F32),
        mine[2 * count + own_cols :],
    )


def solution(mesh):
    in_specs = (
        P(("dp", "mp"), None),
        P("dp", "mp"),
        P("dp", "mp"),
        P("dp", "mp"),
        P("mp", "dp"),
        P("mp", "dp"),
        P("mp", "dp"),
        P("dp"),
        P("dp", "mp"),
        P("dp", "mp"),
        P("mp", "dp"),
        P("dp"),
        P(("dp", "mp"), None),
    )
    out_specs = (
        P(("dp", "mp"), None),
        P(("dp", "mp"), None),
        P("dp", "mp"),
        P("dp", "mp"),
        P("dp", "mp"),
        P("mp", "dp"),
        P("mp", "dp"),
        P("mp", "dp"),
        P("dp"),
        P("dp", "mp"),
        P("dp", "mp"),
        P("mp", "dp"),
        P("dp"),
    )

    def body(*args):
        return local(mesh.shape["mp"], mesh.shape["dp"], *args)

    return jax.shard_map(body, mesh=mesh, in_specs=in_specs, out_specs=out_specs, check_vma=False)
```
